32 devices in a mesh: kpt: 2 (over core), orb: 16 (over z, y, x).
Axes of the slice: x: 2, y: 2, z: 4, core: 2. Of those that a mesh axis runs over, the one named last changes fastest.
Arguments:
- orbitals: bfloat16 [2, 512, 64, 1024], P('kpt', 'orb'), may hold values from -6 to 6
- potential: float32 [64, 1024], replicated, may hold values from 0.5 to 12
Outputs:
- rotated: bfloat16 [2, 512, 64, 1024], P('kpt', 'orb')
- density: float32 [64, 1024], P('orb')
The draws below stay inside these ranges and needn't reach their ends.
All inputs are finite; a program needn't handle non-finite values.
Results may differ from the reference program's by a relative error of at most 0.0068.
The reference program's roundings to bfloat16 on the way (of `tables`, `back`, `filtered` and `coeff`) count: a program that leaves them out, or rounds other values in their place, can miss the bound.
Values may be sent and summed in bfloat16 or wider, within the bound.
No kernel may reach another device: no remote copies, remote signals or barrier semaphores. Data moves between devices by JAX's collectives and lax.ppermute only.
A program may use at most 128 MiB of HBM per device.

```python
import math
import jax
import jax.numpy as jnp
import numpy as np
from jax import lax

NORB = 512
NX = 64
NY = 32
NZ = 32
DEG = 4
ITERS = 8
KPOINTS = 2


def block_scale(stream_key, extent, shards, least, top_value):
    gain = 1.0
    for position, shards_of in shards:
        heights = jax.random.uniform(jax.random.fold_in(jax.random.fold_in(stream_key, 6), position), (shards_of,), jnp.float32, least / len(shards), top_value / len(shards))
        gain = gain * jnp.repeat(jnp.exp(heights), extent[position] // shards_of).reshape((-1,) + (1,) * (len(extent) - 1 - position))
    return gain


def bell_draw(rng, extent, spread, reach, pieces=(), kind=jnp.bfloat16):
    loudness = block_scale(rng, extent, pieces, -0.22, 0.18) if pieces else 1.0
    values = jax.random.normal(rng, extent, jnp.float32) * spread * loudness
    return jnp.minimum(jnp.maximum(values, -reach), reach).astype(kind)


def setup_inputs(seed: int = 0) -> dict:
    streams_of = jax.random.split(jax.random.key(seed), 3)
    return {
        "orbitals": bell_draw(streams_of[0], (KPOINTS, NORB, NX, NY * NZ), 1.0, 6.0, ((0, 2), (1, 16))),
        "potential": jnp.clip(jnp.exp(jax.random.uniform(streams_of[1], (NX, NY * NZ), jnp.float32, math.log(0.5), math.log(12.0))), 0.5, 12.0),
    }


filter_centre = 13.0
filter_half = 9.0
margin_eps = 1e-06

def circulant(taps, first, length):
    matrix = np.zeros((length, length))
    for k in range(len(taps)):
        for i in range(length):
            matrix[i, (i + first + k) % length] += taps[k]
    return matrix

def build_tables(size_x, size_y, size_z):
    kinetic = [math.pi ** 2 / 6.0 if k == 0 else (-1.0) ** k / (k * k) for k in range(-14, 15)]
    smooth_taps = np.array([math.exp(-(k + 0.5) ** 2 / 6.0) for k in range(-8, 8)])
    smooth_taps = smooth_taps / smooth_taps.sum()
    kin_x = circulant(kinetic, -14, size_x)
    mag_x = circulant(smooth_taps, -8, size_x)
    kin_yz = np.kron(circulant(kinetic, -14, size_y), np.eye(size_z)) + np.kron(np.eye(size_y), circulant(kinetic, -14, size_z))
    mag_yz = np.kron(circulant(smooth_taps, -8, size_y), circulant(smooth_taps, -8, size_z))
    yz_table = np.concatenate([kin_yz.T, mag_yz.T], axis=1)
    result = [kin_x, mag_x, mag_x.T, yz_table, mag_yz]
    return [jnp.asarray(table, jnp.float32).astype(jnp.bfloat16) for table in result]

def hamiltonian(block, potential, tables):
    kin_x, mag_x, mag_xt, yz_table, mag_yz = [t.astype(jnp.float32) for t in tables]
    width = block.shape[2]
    hp = lax.Precision.HIGHEST
    value = block.astype(jnp.float32)
    both = jnp.einsum('bxc,cd->bxd', value, yz_table, precision=hp)
    smooth = both[:, :, width:].astype(jnp.bfloat16).astype(jnp.float32)
    kin_all = jnp.einsum('ux,bxc->buc', kin_x, value, precision=hp) + both[:, :, :width]
    weighted = (potential[None] * jnp.einsum('ux,bxc->buc', mag_x, smooth, precision=hp)).astype(jnp.bfloat16).astype(jnp.float32)
    back = jnp.einsum('ux,bxc->buc', mag_xt, weighted, precision=hp).astype(jnp.bfloat16).astype(jnp.float32)
    return kin_all + jnp.einsum('bxc,cd->bxd', back, mag_yz, precision=hp)

def chebyshev(block, potential, tables):
    prev = block
    shifted = hamiltonian(block, potential, tables) - filter_centre * block.astype(jnp.float32)
    now = (shifted / filter_half).astype(jnp.bfloat16)
    for step in range(DEG - 1):
        shifted = hamiltonian(now, potential, tables) - filter_centre * now.astype(jnp.float32)
        nxt = (2.0 * shifted / filter_half - prev.astype(jnp.float32)).astype(jnp.bfloat16)
        prev, now = (now, nxt)
    return now

def reference(orbitals, potential):
    count_kp, count_orb, size_x, width = orbitals.shape
    tables = build_tables(NX, NY, NZ)
    cells = size_x * width
    group = math.gcd(count_orb, 64)
    hp = lax.Precision.HIGHEST
    density = jnp.zeros((cells,), jnp.float32)
    rotated_all = []
    for kp in range(count_kp):
        blocks = orbitals[kp].reshape(count_orb // group, group, size_x, width)
        filtered = lax.map(lambda blk: chebyshev(blk, potential, tables), blocks)
        flat = filtered.reshape(count_orb, cells)
        margin = jnp.dot(flat, flat.T, preferred_element_type=jnp.float32) * (1.0 / cells)
        scale = jnp.sqrt(jnp.sum(margin * margin) + margin_eps)
        eye = jnp.eye(count_orb, dtype=jnp.float32)
        iterate_a = margin / scale
        iterate_z = eye
        for step in range(ITERS):
            factor = 0.5 * (3.0 * eye - jnp.dot(iterate_z, iterate_a, precision=hp))
            iterate_a = jnp.dot(factor, iterate_a, precision=hp)
            iterate_z = jnp.dot(factor, iterate_z, precision=hp)
        coeff = (iterate_z / jnp.sqrt(scale)).astype(jnp.bfloat16)
        rotated = jnp.dot(coeff.T, flat, preferred_element_type=jnp.float32).astype(jnp.bfloat16)
        values = rotated.astype(jnp.float32)
        density = density + lax.optimization_barrier(jnp.sum(values * values, axis=0))
        rotated_all.append(rotated.reshape(count_orb, size_x, width))
    density = density / (count_kp * math.sqrt(count_orb))
    return (jnp.stack(rotated_all, axis=0), density.reshape(size_x, width))
```

```python
import functools
import math

import jax
import jax.numpy as jnp
import numpy as np
from jax import lax
from jax.experimental import pallas as pl
from jax.experimental.pallas import tpu as pltpu
from jax.sharding import PartitionSpec as P

DEG = 4
ITERS = 8
LANES = 128
COLS = 256
CHUNKS = 2
BF = jnp.bfloat16
F32 = jnp.float32

filter_centre = 13.0
filter_half = 9.0
margin_eps = 1e-06


def circulant(taps, first, length):
    matrix = np.zeros((length, length))
    for k in range(len(taps)):
        for i in range(length):
            matrix[i, (i + first + k) % length] += taps[k]
    return matrix


def build_tables(size_x, width):
    side = math.isqrt(width)
    kinetic = [math.pi**2 / 6.0 if k == 0 else (-1.0) ** k / (k * k) for k in range(-14, 15)]
    taps = np.array([math.exp(-((k + 0.5) ** 2) / 6.0) for k in range(-8, 8)])
    taps = taps / taps.sum()
    kin_side = circulant(kinetic, -14, side)
    mag_side = circulant(taps, -8, side)
    kin_yz = np.kron(kin_side, np.eye(side)) + np.kron(np.eye(side), kin_side)
    mag_yz = np.kron(mag_side, mag_side)
    return circulant(kinetic, -14, size_x), circulant(taps, -8, size_x), kin_yz, mag_yz


def to_bf16(table):
    return jnp.asarray(np.asarray(table, np.float32)).astype(BF)


def full_spec(array):
    return pl.BlockSpec(array.shape, lambda *_: (0,) * array.ndim)


def filter_kernel(
    in_ref, pot_ref, kx_ref, mx_ref, mxt_ref, kyz_ref, myz_ref, myzt_ref, out_ref,
    now, prev, smooth, back, nxt, fin, *, bands,
):
    size_x, width = in_ref.shape[1:]
    rows = now.shape[0]
    group = fin.shape[1] // size_x
    step_id = pl.program_id(0)
    blocks = width // COLS
    span = kx_ref.shape[0]
    now[...] = in_ref[...].reshape(rows, width)
    prev[...] = now[...]

    def banded(src, table, n):
        acc = None
        for i, d in enumerate(bands):
            k = (n + d) % blocks
            part = jnp.dot(
                src[:, k * COLS : (k + 1) * COLS],
                table[n, i * COLS : (i + 1) * COLS, :],
                preferred_element_type=F32,
            )
            acc = part if acc is None else acc + part
        return acc

    def step(j, carry):
        gain = jnp.where(j == 0, 1.0 / filter_half, 2.0 / filter_half).astype(F32)
        keep = jnp.where(j == 0, 0.0, 1.0).astype(F32)
        for n in range(blocks):
            cs = slice(n * COLS, (n + 1) * COLS)
            smooth[:, cs] = banded(now, myz_ref, n).astype(BF)
            for r in range(rows // span):
                rs = slice(r * span, (r + 1) * span)
                mixed = jnp.dot(mx_ref[...], smooth[rs, cs], preferred_element_type=F32)
                mixed = mixed.reshape(span // size_x, size_x, COLS) * pot_ref[:, cs][None]
                weighted = mixed.reshape(span, COLS).astype(BF)
                back[rs, cs] = jnp.dot(
                    mxt_ref[...], weighted, preferred_element_type=F32
                ).astype(BF)
        for n in range(blocks):
            cs = slice(n * COLS, (n + 1) * COLS)
            total = jnp.dot(now[...], kyz_ref[:, cs], preferred_element_type=F32)
            total = total + banded(back, myzt_ref, n)
            for r in range(rows // span):
                rs = slice(r * span, (r + 1) * span)
                value = now[rs, cs]
                shifted = (
                    total[rs]
                    + jnp.dot(kx_ref[...], value, preferred_element_type=F32)
                    - filter_centre * value.astype(F32)
                )
                nxt[rs, cs] = (gain * shifted - keep * prev[rs, cs].astype(F32)).astype(BF)
        prev[...] = now[...]
        now[...] = nxt[...]
        return carry

    lax.fori_loop(0, DEG, step, 0)
    for l in range(width // LANES):
        fin[l, pl.ds(pl.multiple_of(step_id * rows, rows), rows), :] = now[
            :, l * LANES : (l + 1) * LANES
        ].astype(F32)

    @pl.when(step_id == pl.num_programs(0) - 1)
    def _():
        per = out_ref.shape[1]
        for x in range(size_x):
            for l in range(width // LANES):
                out_ref[x // per, x % per, :, l * LANES : (l + 1) * LANES] = fin[
                    l, pl.ds(x, group, stride=size_x), :
                ].astype(BF)


def run_filter(orbitals, chunk, potential, parts, rows):
    size_x, width = orbitals.shape[1:]
    group = orbitals.shape[0] // CHUNKS
    rows = min(rows, group * size_x)
    blocks = width // COLS
    kin_x, mag_x, kin_yz, mag_yz = build_tables(size_x, width)
    span = min(256, rows)
    wide = lambda t: to_bf16(np.kron(np.eye(span // size_x), t))
    piece = lambda t, n, d: t[
        n * COLS : (n + 1) * COLS, ((n + d) % blocks) * COLS : ((n + d) % blocks + 1) * COLS
    ]
    bands = [
        d
        for d in range(blocks)
        if any(np.any(piece(t, n, d)) for n in range(blocks) for t in (mag_yz, mag_yz.T))
    ]
    pack = lambda t: to_bf16(
        np.stack(
            [np.concatenate([piece(t, n, d).T for d in bands], 0) for n in range(blocks)]
        )
    )
    args = (
        orbitals, potential, wide(kin_x), wide(mag_x), wide(mag_x.T), to_bf16(kin_yz.T),
        pack(mag_yz), pack(mag_yz.T),
    )
    per = size_x // parts
    steps = group * size_x // rows
    return pl.pallas_call(
        functools.partial(filter_kernel, bands=bands),
        grid=(steps,),
        in_specs=[
            pl.BlockSpec((rows // size_x, size_x, width), lambda s: (chunk * steps + s, 0, 0))
        ]
        + [full_spec(a) for a in args[1:]],
        out_specs=pl.BlockSpec((parts, per, group, width), lambda s: (0, 0, 0, 0)),
        out_shape=jax.ShapeDtypeStruct((parts, per, group, width), BF),
        scratch_shapes=[pltpu.VMEM((rows, width), BF)] * 5
        + [pltpu.VMEM((width // LANES, group * size_x, LANES), F32)],
        compiler_params=pltpu.CompilerParams(vmem_limit_bytes=56 << 20),
        cost_estimate=pl.CostEstimate(
            flops=2 * DEG * group * size_x * width * (width + 2 * len(bands) * COLS + 3 * span),
            bytes_accessed=4 * group * size_x * width,
            transcendentals=0,
        ),
        name="chebyshev",
    )(*args)


def triangle(count, side):
    n = count // side
    return [(i, j) for i in range(n) for j in range(i, n)]


def margin_kernel(*refs, side, gain):
    ins, out_ref, flat = refs[:-2], refs[-2], refs[-1]
    step_id = pl.program_id(0)
    width = flat.shape[1]
    start = 0
    for ref in ins:
        size = ref.shape[0] * ref.shape[2]
        flat[start : start + size, :] = ref[:, 0].reshape(size, width)
        start += size
    n = start // side

    @pl.when(step_id == 0)
    def _():
        out_ref[...] = jnp.zeros_like(out_ref)

    at = 0
    for i in range(n):
        got = lax.dot_general(
            flat[i * side : (i + 1) * side, :],
            flat[i * side :, :],
            (((1,), (1,)), ((), ())),
            preferred_element_type=F32,
        )
        for j in range(n - i):
            rs = slice((at + j) * side, (at + j + 1) * side)
            out_ref[rs, :] += got[:, j * side : (j + 1) * side]
        at += n - i

    @pl.when(step_id == pl.num_programs(0) - 1)
    def _():
        out_ref[...] = out_ref[...] * gain


def run_margin(spreads, cells, side):
    parts, per, _, width = spreads[0].shape
    count = sum(s.shape[0] * s.shape[2] for s in spreads)
    shape = (len(triangle(count, side)) * side, side)
    return pl.pallas_call(
        functools.partial(margin_kernel, side=side, gain=1.0 / cells),
        grid=(per,),
        in_specs=[
            pl.BlockSpec((parts, 1, s.shape[2], width), lambda x: (0, x, 0, 0)) for s in spreads
        ],
        out_specs=pl.BlockSpec(shape, lambda x: (0, 0)),
        out_shape=jax.ShapeDtypeStruct(shape, F32),
        scratch_shapes=[pltpu.VMEM((count, width), BF)],
        compiler_params=pltpu.CompilerParams(vmem_limit_bytes=48 << 20),
        cost_estimate=pl.CostEstimate(
            flops=count * count * width * per, bytes_accessed=2 * count * width * per,
            transcendentals=0,
        ),
        name="margin",
    )(*spreads)


def reduce_margin(partial, parts):
    size, side = partial.shape
    pieces = lax.all_to_all(
        partial.reshape(parts, size // parts, side), "orb", split_axis=0, concat_axis=0, tiled=True
    )
    held = jnp.sum(pieces, axis=0)[None]
    masks = [0]
    bit = parts // 2
    while bit:
        other = lax.ppermute(held, "orb", [(i, i ^ bit) for i in range(parts)])
        held = jnp.concatenate([held, other], axis=0)
        masks = masks + [m ^ bit for m in masks]
        bit //= 2
    return held, masks


def split(value):
    high = value.astype(BF)
    return high, (value - high.astype(F32)).astype(BF)


def mul(a, b):
    ah, al = a
    bh, bl = b
    dot = functools.partial(jnp.dot, preferred_element_type=F32)
    return dot(ah, bh) + (dot(ah, bl) + dot(al, bh))


def inverse_root_kernel(me_ref, held_ref, out_ref, packed, full, *, masks, side):
    me = me_ref[0]
    piece = held_ref.shape[1]
    for t, m in enumerate(masks):
        packed[pl.ds(pl.multiple_of((me ^ m) * piece, math.gcd(piece, 8)), piece), :] = held_ref[t]
    count = full.shape[0]
    for at, (i, j) in enumerate(triangle(count, side)):
        tile = packed[at * side : (at + 1) * side, :]
        full[i * side : (i + 1) * side, j * side : (j + 1) * side] = tile
        if i != j:
            full[j * side : (j + 1) * side, i * side : (i + 1) * side] = tile.T
    margin = full[...]
    total = jnp.sum(jnp.sum(margin * margin, axis=1, keepdims=True), axis=0, keepdims=True)
    scale = jnp.sqrt(total + margin_eps)
    row = lax.broadcasted_iota(jnp.int32, (count, count), 0)
    col = lax.broadcasted_iota(jnp.int32, (count, count), 1)
    eye = jnp.where(row == col, 1.0, 0.0).astype(F32)
    p = margin / scale
    z = None
    for pair in range(ITERS // 2):
        ps = split(p)
        square = mul(ps, ps)
        inner = 6.75 * eye - 2.25 * p + 0.25 * square
        w = 0.25 * (9.0 * eye - 9.75 * p + mul(split(square), split(inner)))
        ws = split(w)
        z = w if z is None else mul(ws, split(z))
        if pair < ITERS // 2 - 1:
            p = mul(ws, split(mul(ws, ps)))
    out_ref[...] = (z / jnp.sqrt(scale)).astype(BF)


def run_inverse_root(held, masks, count, side):
    me = lax.axis_index("orb").astype(jnp.int32).reshape(1)
    return pl.pallas_call(
        functools.partial(inverse_root_kernel, masks=masks, side=side),
        in_specs=[
            pl.BlockSpec(memory_space=pltpu.SMEM),
            pl.BlockSpec(memory_space=pltpu.VMEM),
        ],
        out_specs=pl.BlockSpec(memory_space=pltpu.VMEM),
        out_shape=jax.ShapeDtypeStruct((count, count), BF),
        scratch_shapes=[
            pltpu.VMEM((held.shape[0] * held.shape[1], side), F32),
            pltpu.VMEM((count, count), F32),
        ],
        compiler_params=pltpu.CompilerParams(vmem_limit_bytes=48 << 20),
        cost_estimate=pl.CostEstimate(
            flops=2 * 51 * count**3, bytes_accessed=4 * count * count, transcendentals=0
        ),
        name="inverse_root",
    )(me, held)


def rotate_kernel(*refs):
    coeff_ref, ins, out_ref, den_ref, flat = refs[0], refs[1:-3], refs[-3], refs[-2], refs[-1]
    width = flat.shape[1]
    start = 0
    for ref in ins:
        size = ref.shape[0] * ref.shape[2]
        flat[start : start + size, :] = ref[:, 0].reshape(size, width)
        start += size
    value = jnp.dot(coeff_ref[...], flat[...], preferred_element_type=F32).astype(BF)
    out_ref[:, 0] = value.reshape(out_ref.shape[0], out_ref.shape[2], width)
    wide = value.astype(F32)
    den_ref[...] = jnp.sum(wide * wide, axis=0)[None, None]


def run_rotate(coeff, spreads):
    parts, per, group, width = spreads[0].shape
    count = coeff.shape[1]
    return pl.pallas_call(
        rotate_kernel,
        grid=(per,),
        in_specs=[full_spec(coeff)]
        + [pl.BlockSpec((parts, 1, s.shape[2], width), lambda x: (0, x, 0, 0)) for s in spreads],
        out_specs=[
            pl.BlockSpec((parts, 1, group, width), lambda x: (0, x, 0, 0)),
            pl.BlockSpec((1, 1, width), lambda x: (x, 0, 0)),
        ],
        out_shape=[
            jax.ShapeDtypeStruct((parts, per, group, width), BF),
            jax.ShapeDtypeStruct((per, 1, width), F32),
        ],
        scratch_shapes=[pltpu.VMEM((count, width), BF)],
        compiler_params=pltpu.CompilerParams(vmem_limit_bytes=48 << 20),
        cost_estimate=pl.CostEstimate(
            flops=2 * count * parts * group * width * per,
            bytes_accessed=2 * (count + parts * group) * width * per,
            transcendentals=0,
        ),
        name="rotate",
    )(coeff, *spreads)


def restore_kernel(*refs):
    in_ref, out_ref, wide = refs[0], refs[-2], refs[-1]
    parts, per, group, _ = in_ref.shape
    for s in range(parts):
        for x in range(per):
            wide[pl.ds((s * per + x) * group, group), :] = in_ref[s, x].astype(F32)
    for g in range(group):
        out_ref[g] = wide[pl.ds(g, parts * per, stride=group), :].astype(BF)


def run_restore(spread, target, chunk, chunks):
    parts, per, group, width = spread.shape
    size_x = parts * per
    args = (spread,) if target is None else (spread, target)
    return pl.pallas_call(
        restore_kernel,
        grid=(width // LANES,),
        in_specs=[pl.BlockSpec((parts, per, group, LANES), lambda l: (0, 0, 0, l))]
        + [pl.BlockSpec(memory_space=pl.ANY)] * (len(args) - 1),
        out_specs=pl.BlockSpec((group, size_x, LANES), lambda l: (chunk, 0, l)),
        out_shape=jax.ShapeDtypeStruct((group * chunks, size_x, width), BF),
        scratch_shapes=[pltpu.VMEM((size_x * group, LANES), F32)],
        input_output_aliases={} if target is None else {1: 0},
        cost_estimate=pl.CostEstimate(
            flops=0, bytes_accessed=4 * group * size_x * width, transcendentals=0
        ),
        name="restore",
    )(*args)


def shards(orbitals, potential):
    parts = lax.axis_size("orb")
    mine, size_x, width = orbitals.shape[1:]
    group = mine // CHUNKS
    count = mine * parts
    exchange = lambda v: lax.all_to_all(v, "orb", split_axis=0, concat_axis=0, tiled=True)
    spreads = []
    for c in range(CHUNKS):
        spreads.append(exchange(run_filter(orbitals[0], c, potential, parts, 1024)))
    partial = run_margin(spreads, size_x * width, LANES)
    held, masks = reduce_margin(partial, parts)
    coeff = run_inverse_root(held, masks, count, LANES)
    own = group * parts
    target = None
    density = 0.0
    returned = []
    for c in range(CHUNKS):
        rotated, part = run_rotate(coeff[c * own : (c + 1) * own], spreads)
        returned.append(exchange(rotated))
        density = density + part[:, 0]
    for c in range(CHUNKS):
        target = run_restore(returned[c], target, c, CHUNKS)
    kpoints = lax.axis_size("kpt")
    total = density
    for k in range(1, kpoints):
        total = total + lax.ppermute(
            density, "kpt", [(i, (i + k) % kpoints) for i in range(kpoints)]
        )
    weight = 1.0 / (kpoints * math.sqrt(count))
    return target[None], total * weight


def solution(mesh):
    in_specs = (P("kpt", "orb", None, None), P())
    out_specs = (P("kpt", "orb", None, None), P("orb", None))
    return jax.shard_map(shards, mesh=mesh, in_specs=in_specs, out_specs=out_specs, check_vma=False)
```

```python
import functools
import math

import jax
import jax.numpy as jnp
import numpy as np
from jax import lax
from jax.experimental import pallas as pl
from jax.experimental.pallas import tpu as pltpu
from jax.sharding import PartitionSpec as P

DEG = 4
ITERS = 8
LANES = 128
COLS = 256
CHUNKS = 2
BF = jnp.bfloat16
F32 = jnp.float32

filter_centre = 13.0
filter_half = 9.0
margin_eps = 1e-06


def circulant(taps, first, length):
    matrix = np.zeros((length, length))
    for k in range(len(taps)):
        for i in range(length):
            matrix[i, (i + first + k) % length] += taps[k]
    return matrix


def build_tables(size_x, width):
    side = math.isqrt(width)
    kinetic = [math.pi**2 / 6.0 if k == 0 else (-1.0) ** k / (k * k) for k in range(-14, 15)]
    taps = np.array([math.exp(-((k + 0.5) ** 2) / 6.0) for k in range(-8, 8)])
    taps = taps / taps.sum()
    kin_side = circulant(kinetic, -14, side)
    mag_side = circulant(taps, -8, side)
    kin_yz = np.kron(kin_side, np.eye(side)) + np.kron(np.eye(side), kin_side)
    mag_yz = np.kron(mag_side, mag_side)
    return circulant(kinetic, -14, size_x), circulant(taps, -8, size_x), kin_yz, mag_yz


def to_bf16(table):
    return jnp.asarray(np.asarray(table, np.float32)).astype(BF)


def full_spec(array):
    return pl.BlockSpec(array.shape, lambda *_: (0,) * array.ndim)


def filter_kernel(
    in_ref, pot_ref, kx_ref, mx_ref, kyz_ref, myz_ref, myzt_ref, out_ref,
    now, prev, smooth, mixed, back, nxt, fin, mxt_ref, *, first, firstt,
):
    size_x, width = in_ref.shape[1:]
    rows = now.shape[0]
    group = fin.shape[0] // size_x
    step_id = pl.program_id(0)
    blocks = width // COLS
    span = kx_ref.shape[0]
    tiles = [
        (slice(r, r + span), slice(c, c + COLS))
        for c in range(0, width, COLS)
        for r in range(0, rows, span)
    ]
    dot = functools.partial(jnp.dot, preferred_element_type=F32)
    mxt_ref[...] = mx_ref[...].astype(F32).T.astype(BF)
    start = in_ref[...].reshape(rows, width)
    now[:, :width] = start
    now[:, width:] = start
    prev[...] = start

    def window(src, table, n, lead):
        at = (n + lead) % blocks * COLS
        return dot(src[:, at : at + table.shape[0]], table[...])

    def step(j, carry):
        gain = jnp.where(j == 0, 1.0 / filter_half, 2.0 / filter_half).astype(F32)
        keep = jnp.where(j == 0, 0.0, 1.0).astype(F32)
        for n in range(blocks):
            smooth[:, n * COLS : (n + 1) * COLS] = window(now, myz_ref, n, first).astype(BF)
        for rs, cs in tiles:
            value = dot(mx_ref[...], smooth[rs, cs])
            value = value.reshape(span // size_x, size_x, COLS) * pot_ref[:, cs][None]
            mixed[rs, cs] = value.reshape(span, COLS).astype(BF)
        for rs, cs in tiles:
            value = dot(mxt_ref[...], mixed[rs, cs]).astype(BF)
            back[rs, cs] = value
            back[rs, cs.start + width : cs.stop + width] = value
        for n in range(blocks):
            cs = slice(n * COLS, (n + 1) * COLS)
            total = window(now, kyz_ref, n, 0) + window(back, myzt_ref, n, firstt)
            for r in range(0, rows, span):
                rs = slice(r, r + span)
                value = now[rs, cs]
                shifted = total[rs] + dot(kx_ref[...], value) - filter_centre * value.astype(F32)
                nxt[rs, cs] = (gain * shifted - keep * prev[rs, cs].astype(F32)).astype(BF)
        prev[...] = now[:, :width]
        now[:, :width] = nxt[...]
        now[:, width:] = nxt[...]
        return carry

    lax.fori_loop(0, DEG, step, 0)
    fin[pl.ds(pl.multiple_of(step_id * rows, rows), rows), :] = nxt[...]

    @pl.when(step_id == pl.num_programs(0) - 1)
    def _():
        turned = jnp.swapaxes(fin[...].reshape(group, size_x, width), 0, 1)
        out_ref[...] = turned.reshape(out_ref.shape)


def run_filter(orbitals, chunk, potential, parts, rows):
    size_x, width = orbitals.shape[1:]
    group = orbitals.shape[0] // CHUNKS
    rows = min(rows, group * size_x)
    blocks = width // COLS
    kin_x, mag_x, kin_yz, mag_yz = build_tables(size_x, width)
    span = min(256, rows)
    wide = lambda t: to_bf16(np.kron(np.eye(span // size_x), t))
    piece = lambda t, d: t[:COLS, d % blocks * COLS : (d % blocks + 1) * COLS].T

    def band(t):
        used = [d for d in range(blocks) if np.any(piece(t, d))]
        lead = [d for d in used if (d - 1) % blocks not in used]
        lead = lead[0] if lead else 0
        return lead, to_bf16(np.concatenate([piece(t, lead + i) for i in range(len(used))], 0))

    _, kyz = band(kin_yz)
    first, myz = band(mag_yz)
    firstt, myzt = band(mag_yz.T)
    args = (orbitals, potential, wide(kin_x), wide(mag_x), kyz, myz, myzt)
    per = size_x // parts
    steps = group * size_x // rows
    return pl.pallas_call(
        functools.partial(filter_kernel, first=first, firstt=firstt),
        grid=(steps,),
        in_specs=[
            pl.BlockSpec((rows // size_x, size_x, width), lambda s: (chunk * steps + s, 0, 0))
        ]
        + [full_spec(a) for a in args[1:]],
        out_specs=pl.BlockSpec((parts, per, group, width), lambda s: (0, 0, 0, 0)),
        out_shape=jax.ShapeDtypeStruct((parts, per, group, width), BF),
        scratch_shapes=[
            pltpu.VMEM((rows, 2 * width), BF),
            pltpu.VMEM((rows, width), BF),
            pltpu.VMEM((rows, width), BF),
            pltpu.VMEM((rows, width), BF),
            pltpu.VMEM((rows, 2 * width), BF),
            pltpu.VMEM((rows, width), BF),
            pltpu.VMEM((group * size_x, width), BF),
            pltpu.VMEM((span, span), BF),
        ],
        compiler_params=pltpu.CompilerParams(vmem_limit_bytes=56 << 20),
        cost_estimate=pl.CostEstimate(
            flops=2 * DEG * group * size_x * width
            * (kyz.shape[0] + myz.shape[0] + myzt.shape[0] + 3 * span),
            bytes_accessed=4 * group * size_x * width,
            transcendentals=0,
        ),
        name="chebyshev",
    )(*args)


def triangle(count, side):
    n = count // side
    return [(i, j) for i in range(n) for j in range(i, n)]


def margin_kernel(me_ref, *refs, side, gain, order):
    ins, out_ref, flat, acc = refs[:-3], refs[-3], refs[-2], refs[-1]
    step_id = pl.program_id(0)
    width = flat.shape[1]
    start = 0
    for ref in ins:
        size = ref.shape[0] * ref.shape[2]
        flat[start : start + size, :] = ref[:, 0].reshape(size, width)
        start += size
    n = start // side

    @pl.when(step_id == 0)
    def _():
        acc[...] = jnp.zeros_like(acc)

    at = 0
    for i in range(n):
        got = lax.dot_general(
            flat[i * side : (i + 1) * side, :],
            flat[i * side :, :],
            (((1,), (1,)), ((), ())),
            preferred_element_type=F32,
        )
        for j in range(n - i):
            rs = slice((at + j) * side, (at + j + 1) * side)
            acc[rs, :] += got[:, j * side : (j + 1) * side]
        at += n - i

    @pl.when(step_id == pl.num_programs(0) - 1)
    def _():
        piece = out_ref.shape[1]
        for t, m in enumerate(order):
            rows = pl.multiple_of((me_ref[0] ^ m) * piece, math.gcd(piece, 8))
            out_ref[t] = acc[pl.ds(rows, piece), :] * gain


def run_margin(me, spreads, cells, side, order):
    parts, per, _, width = spreads[0].shape
    count = sum(s.shape[0] * s.shape[2] for s in spreads)
    size = len(triangle(count, side)) * side
    shape = (parts, size // parts, side)
    return pl.pallas_call(
        functools.partial(margin_kernel, side=side, gain=1.0 / cells, order=order),
        grid=(per,),
        in_specs=[pl.BlockSpec(memory_space=pltpu.SMEM)]
        + [pl.BlockSpec((parts, 1, s.shape[2], width), lambda x: (0, x, 0, 0)) for s in spreads],
        out_specs=pl.BlockSpec(shape, lambda x: (0, 0, 0)),
        out_shape=jax.ShapeDtypeStruct(shape, F32),
        scratch_shapes=[pltpu.VMEM((count, width), BF), pltpu.VMEM((size, side), F32)],
        compiler_params=pltpu.CompilerParams(vmem_limit_bytes=48 << 20),
        cost_estimate=pl.CostEstimate(
            flops=count * count * width * per, bytes_accessed=2 * count * width * per,
            transcendentals=0,
        ),
        name="margin",
    )(me, *spreads)


def stage_masks(parts):
    stages, low = [], 1
    while low < parts:
        bits = [low, 2 * low] if 2 * low < parts else [low]
        masks = [0]
        for b in bits:
            masks += [m ^ b for m in masks]
        stages.append(masks)
        low <<= len(bits)
    return stages


def piece_order(stages):
    order = [0]
    for masks in reversed(stages):
        order = [m ^ o for m in masks for o in order]
    return order


def send(value, mask, parts):
    return lax.ppermute(value, "orb", [(i, i ^ mask) for i in range(parts)])


def reduce_margin(held, stages, parts):
    for masks in stages:
        held = held.reshape((len(masks), -1) + held.shape[1:])
        total = held[0]
        for other in [send(held[i], m, parts) for i, m in enumerate(masks) if i]:
            total = total + other
        held = total
    for masks in reversed(stages):
        got = [send(held, m, parts) for m in masks[1:]]
        held = jnp.concatenate([held] + got, axis=0)
    return held


def split(value):
    high = value.astype(BF)
    return high, (value - high.astype(F32)).astype(BF)


def mul(a, b):
    ah, al = a
    bh, bl = b
    dot = functools.partial(jnp.dot, preferred_element_type=F32)
    return dot(ah, bh) + (dot(ah, bl) + dot(al, bh))


def inverse_root_kernel(
    me_ref, held_ref, out_ref, packed, full, pval, zhi, zlo, *, masks, side
):
    me = me_ref[0]
    piece = held_ref.shape[1]
    for t, m in enumerate(masks):
        packed[pl.ds(pl.multiple_of((me ^ m) * piece, math.gcd(piece, 8)), piece), :] = held_ref[t]
    count = full.shape[0]
    for at, (i, j) in enumerate(triangle(count, side)):
        tile = packed[at * side : (at + 1) * side, :]
        full[i * side : (i + 1) * side, j * side : (j + 1) * side] = tile
        if i != j:
            full[j * side : (j + 1) * side, i * side : (i + 1) * side] = tile.T
    margin = full[...]
    total = jnp.sum(jnp.sum(margin * margin, axis=1, keepdims=True), axis=0, keepdims=True)
    scale = jnp.sqrt(total + margin_eps)
    row = lax.broadcasted_iota(jnp.int32, (count, count), 0)
    col = lax.broadcasted_iota(jnp.int32, (count, count), 1)
    eye = jnp.where(row == col, 1.0, 0.0).astype(F32)

    def factor(ps, p):
        square = mul(ps, ps)
        inner = 6.75 * eye - 2.25 * p + 0.25 * square
        return 0.25 * (9.0 * eye - 9.75 * p + mul(split(square), split(inner)))

    def pair(p, last):
        ps = split(p)
        ws = split(factor(ps, p))
        return ws, None if last else mul(ws, split(mul(ws, ps)))

    ws, pval[...] = pair(margin / scale, False)
    zhi[...], zlo[...] = ws

    def middle(_, carry):
        ws, pval[...] = pair(pval[...], False)
        zhi[...], zlo[...] = split(mul(ws, (zhi[...], zlo[...])))
        return carry

    lax.fori_loop(0, ITERS // 2 - 2, middle, 0)
    ws, _ = pair(pval[...], True)
    z = mul(ws, (zhi[...], zlo[...]))
    out_ref[...] = (z / jnp.sqrt(scale)).astype(BF)


def run_inverse_root(me, held, masks, count, side):
    return pl.pallas_call(
        functools.partial(inverse_root_kernel, masks=masks, side=side),
        in_specs=[
            pl.BlockSpec(memory_space=pltpu.SMEM),
            pl.BlockSpec(memory_space=pltpu.VMEM),
        ],
        out_specs=pl.BlockSpec(memory_space=pltpu.VMEM),
        out_shape=jax.ShapeDtypeStruct((count, count), BF),
        scratch_shapes=[
            pltpu.VMEM((held.shape[0] * held.shape[1], side), F32),
            pltpu.VMEM((count, count), F32),
            pltpu.VMEM((count, count), F32),
            pltpu.VMEM((count, count), BF),
            pltpu.VMEM((count, count), BF),
        ],
        compiler_params=pltpu.CompilerParams(vmem_limit_bytes=48 << 20),
        cost_estimate=pl.CostEstimate(
            flops=2 * 51 * count**3, bytes_accessed=4 * count * count, transcendentals=0
        ),
        name="inverse_root",
    )(me, held)


def rotate_kernel(*refs):
    coeff_ref, ins, out_ref, den_ref, flat = refs[0], refs[1:-3], refs[-3], refs[-2], refs[-1]
    width = flat.shape[1]
    start = 0
    for ref in ins:
        size = ref.shape[0] * ref.shape[2]
        flat[start : start + size, :] = ref[:, 0].reshape(size, width)
        start += size
    value = jnp.dot(coeff_ref[...], flat[...], preferred_element_type=F32).astype(BF)
    out_ref[:, 0] = value.reshape(out_ref.shape[0], out_ref.shape[2], width)
    wide = value.astype(F32)
    den_ref[...] = jnp.sum(wide * wide, axis=0)[None, None]


def run_rotate(coeff, spreads):
    parts, per, group, width = spreads[0].shape
    count = coeff.shape[1]
    return pl.pallas_call(
        rotate_kernel,
        grid=(per,),
        in_specs=[full_spec(coeff)]
        + [pl.BlockSpec((parts, 1, s.shape[2], width), lambda x: (0, x, 0, 0)) for s in spreads],
        out_specs=[
            pl.BlockSpec((parts, 1, group, width), lambda x: (0, x, 0, 0)),
            pl.BlockSpec((1, 1, width), lambda x: (x, 0, 0)),
        ],
        out_shape=[
            jax.ShapeDtypeStruct((parts, per, group, width), BF),
            jax.ShapeDtypeStruct((per, 1, width), F32),
        ],
        scratch_shapes=[pltpu.VMEM((count, width), BF)],
        compiler_params=pltpu.CompilerParams(vmem_limit_bytes=48 << 20),
        cost_estimate=pl.CostEstimate(
            flops=2 * count * parts * group * width * per,
            bytes_accessed=2 * (count + parts * group) * width * per,
            transcendentals=0,
        ),
        name="rotate",
    )(coeff, *spreads)


def restore_kernel(*refs):
    in_ref, out_ref, wide = refs[0], refs[-2], refs[-1]
    parts, per, group, _ = in_ref.shape
    for s in range(parts):
        for x in range(per):
            wide[pl.ds((s * per + x) * group, group), :] = in_ref[s, x].astype(F32)
    for g in range(group):
        out_ref[g] = wide[pl.ds(g, parts * per, stride=group), :].astype(BF)


def run_restore(spread, target, chunk, chunks):
    parts, per, group, width = spread.shape
    size_x = parts * per
    args = (spread,) if target is None else (spread, target)
    return pl.pallas_call(
        restore_kernel,
        grid=(width // LANES,),
        in_specs=[pl.BlockSpec((parts, per, group, LANES), lambda l: (0, 0, 0, l))]
        + [pl.BlockSpec(memory_space=pl.ANY)] * (len(args) - 1),
        out_specs=pl.BlockSpec((group, size_x, LANES), lambda l: (chunk, 0, l)),
        out_shape=jax.ShapeDtypeStruct((group * chunks, size_x, width), BF),
        scratch_shapes=[pltpu.VMEM((size_x * group, LANES), F32)],
        input_output_aliases={} if target is None else {1: 0},
        cost_estimate=pl.CostEstimate(
            flops=0, bytes_accessed=4 * group * size_x * width, transcendentals=0
        ),
        name="restore",
    )(*args)


def shards(orbitals, potential):
    parts = lax.axis_size("orb")
    mine, size_x, width = orbitals.shape[1:]
    group = mine // CHUNKS
    count = mine * parts
    exchange = lambda v: lax.all_to_all(v, "orb", split_axis=0, concat_axis=0, tiled=True)
    spreads = []
    for c in range(CHUNKS):
        spreads.append(exchange(run_filter(orbitals[0], c, potential, parts, 512)))
    me = lax.axis_index("orb").astype(jnp.int32).reshape(1)
    stages = stage_masks(parts)
    order = piece_order(stages)
    partial = run_margin(me, spreads, size_x * width, LANES, order)
    held = reduce_margin(partial, stages, parts)
    coeff = run_inverse_root(me, held, order, count, LANES)
    own = group * parts
    target = None
    density = 0.0
    returned = []
    for c in range(CHUNKS):
        rotated, part = run_rotate(coeff[c * own : (c + 1) * own], spreads)
        returned.append(exchange(rotated))
        density = density + part[:, 0]
    for c in range(CHUNKS):
        target = run_restore(returned[c], target, c, CHUNKS)
    kpoints = lax.axis_size("kpt")
    total = density
    for k in range(1, kpoints):
        total = total + lax.ppermute(
            density, "kpt", [(i, (i + k) % kpoints) for i in range(kpoints)]
        )
    weight = 1.0 / (kpoints * math.sqrt(count))
    return target[None], total * weight


def solution(mesh):
    in_specs = (P("kpt", "orb", None, None), P())
    out_specs = (P("kpt", "orb", None, None), P("orb", None))
    return jax.shard_map(shards, mesh=mesh, in_specs=in_specs, out_specs=out_specs, check_vma=False)
```

```python
import functools
import math

import jax
import jax.numpy as jnp
import numpy as np
from jax import lax
from jax.experimental import pallas as pl
from jax.experimental.pallas import tpu as pltpu
from jax.sharding import PartitionSpec as P

DEG = 4
ITERS = 8
LANES = 128
COLS = 256
OUT_CHUNKS = 2
BF = jnp.bfloat16
F32 = jnp.float32

filter_centre = 13.0
filter_half = 9.0
margin_eps = 1e-06


def circulant(taps, first, length):
    matrix = np.zeros((length, length))
    for k in range(len(taps)):
        for i in range(length):
            matrix[i, (i + first + k) % length] += taps[k]
    return matrix


def build_tables(size_x, width):
    side = math.isqrt(width)
    kinetic = [math.pi**2 / 6.0 if k == 0 else (-1.0) ** k / (k * k) for k in range(-14, 15)]
    taps = np.array([math.exp(-((k + 0.5) ** 2) / 6.0) for k in range(-8, 8)])
    taps = taps / taps.sum()
    kin_side = circulant(kinetic, -14, side)
    mag_side = circulant(taps, -8, side)
    kin_yz = np.kron(kin_side, np.eye(side)) + np.kron(np.eye(side), kin_side)
    mag_yz = np.kron(mag_side, mag_side)
    return circulant(kinetic, -14, size_x), circulant(taps, -8, size_x), kin_yz, mag_yz


def to_bf16(table):
    return jnp.asarray(np.asarray(table, np.float32)).astype(BF)


def full_spec(array):
    return pl.BlockSpec(array.shape, lambda *_: (0,) * array.ndim)


def filter_kernel(
    in_ref, pot_ref, kx_ref, mx_ref, kyz_ref, myz_ref, myzt_ref, out_ref,
    now, prev, smooth, mixed, back, nxt, fin, mxt_ref, *, first, firstt,
):
    size_x, width = in_ref.shape[1:]
    rows = now.shape[0]
    group = fin.shape[0] // size_x
    step_id = pl.program_id(0)
    blocks = width // COLS
    span = kx_ref.shape[0]
    tiles = [
        (slice(r, r + span), slice(c, c + COLS))
        for c in range(0, width, COLS)
        for r in range(0, rows, span)
    ]
    dot = functools.partial(jnp.dot, preferred_element_type=F32)
    mxt_ref[...] = mx_ref[...].astype(F32).T.astype(BF)
    start = in_ref[...].reshape(rows, width)
    now[:, :width] = start
    now[:, width:] = start
    prev[...] = start

    def window(src, table, n, lead):
        at = (n + lead) % blocks * COLS
        return dot(src[:, at : at + table.shape[0]], table[...])

    def step(j, carry):
        gain = jnp.where(j == 0, 1.0 / filter_half, 2.0 / filter_half).astype(F32)
        keep = jnp.where(j == 0, 0.0, 1.0).astype(F32)
        for n in range(blocks):
            smooth[:, n * COLS : (n + 1) * COLS] = window(now, myz_ref, n, first).astype(BF)
        for rs, cs in tiles:
            value = dot(mx_ref[...], smooth[rs, cs])
            value = value.reshape(span // size_x, size_x, COLS) * pot_ref[:, cs][None]
            mixed[rs, cs] = value.reshape(span, COLS).astype(BF)
        for rs, cs in tiles:
            value = dot(mxt_ref[...], mixed[rs, cs]).astype(BF)
            back[rs, cs] = value
            back[rs, cs.start + width : cs.stop + width] = value
        for n in range(blocks):
            cs = slice(n * COLS, (n + 1) * COLS)
            total = window(now, kyz_ref, n, 0) + window(back, myzt_ref, n, firstt)
            for r in range(0, rows, span):
                rs = slice(r, r + span)
                value = now[rs, cs]
                shifted = total[rs] + dot(kx_ref[...], value) - filter_centre * value.astype(F32)
                nxt[rs, cs] = (gain * shifted - keep * prev[rs, cs].astype(F32)).astype(BF)
        prev[...] = now[:, :width]
        now[:, :width] = nxt[...]
        now[:, width:] = nxt[...]
        return carry

    lax.fori_loop(0, DEG, step, 0)
    fin[pl.ds(pl.multiple_of(step_id * rows, rows), rows), :] = nxt[...]

    @pl.when(step_id == pl.num_programs(0) - 1)
    def _():
        turned = jnp.swapaxes(fin[...].reshape(group, size_x, width), 0, 1)
        out_ref[...] = turned.reshape(out_ref.shape)


def run_filter(orbitals, chunk, chunks, potential, parts, rows):
    size_x, width = orbitals.shape[1:]
    group = orbitals.shape[0] // chunks
    rows = min(rows, group * size_x)
    blocks = width // COLS
    kin_x, mag_x, kin_yz, mag_yz = build_tables(size_x, width)
    span = min(256, rows)
    wide = lambda t: to_bf16(np.kron(np.eye(span // size_x), t))
    piece = lambda t, d: t[:COLS, d % blocks * COLS : (d % blocks + 1) * COLS].T

    def band(t):
        used = [d for d in range(blocks) if np.any(piece(t, d))]
        lead = [d for d in used if (d - 1) % blocks not in used]
        lead = lead[0] if lead else 0
        return lead, to_bf16(np.concatenate([piece(t, lead + i) for i in range(len(used))], 0))

    _, kyz = band(kin_yz)
    first, myz = band(mag_yz)
    firstt, myzt = band(mag_yz.T)
    args = (orbitals, potential, wide(kin_x), wide(mag_x), kyz, myz, myzt)
    per = size_x // parts
    steps = group * size_x // rows
    return pl.pallas_call(
        functools.partial(filter_kernel, first=first, firstt=firstt),
        grid=(steps,),
        in_specs=[
            pl.BlockSpec((rows // size_x, size_x, width), lambda s: (chunk * steps + s, 0, 0))
        ]
        + [full_spec(a) for a in args[1:]],
        out_specs=pl.BlockSpec((parts, per, group, width), lambda s: (0, 0, 0, 0)),
        out_shape=jax.ShapeDtypeStruct((parts, per, group, width), BF),
        scratch_shapes=[
            pltpu.VMEM((rows, 2 * width), BF),
            pltpu.VMEM((rows, width), BF),
            pltpu.VMEM((rows, width), BF),
            pltpu.VMEM((rows, width), BF),
            pltpu.VMEM((rows, 2 * width), BF),
            pltpu.VMEM((rows, width), BF),
            pltpu.VMEM((group * size_x, width), BF),
            pltpu.VMEM((span, span), BF),
        ],
        compiler_params=pltpu.CompilerParams(vmem_limit_bytes=56 << 20),
        cost_estimate=pl.CostEstimate(
            flops=2 * DEG * group * size_x * width
            * (kyz.shape[0] + myz.shape[0] + myzt.shape[0] + 3 * span),
            bytes_accessed=4 * group * size_x * width,
            transcendentals=0,
        ),
        name="chebyshev",
    )(*args)


def triangle(count, side):
    n = count // side
    return [(i, j) for i in range(n) for j in range(i, n)]


def gather_rows(ins, flat):
    start = 0
    for ref in ins:
        size = ref.shape[0] * ref.shape[2]
        flat[start : start + size, :] = (
            ref[:, 0].astype(F32).reshape(size, flat.shape[1]).astype(BF)
        )
        start += size


def margin_kernel(me_ref, *refs, side, gain, order, blocks, sources):
    ins, out_ref, flat, acc = refs[:sources], refs[-3], refs[-2], refs[-1]
    step_id = pl.program_id(0)
    gather_rows(ins, flat)

    @pl.when(step_id == 0)
    def _():
        acc[...] = jnp.zeros_like(acc)

    for i in sorted({i for i, _ in blocks}):
        cols = [j for b, j in blocks if b == i]
        got = lax.dot_general(
            flat[i * side : (i + 1) * side, :],
            flat[cols[0] * side : (cols[-1] + 1) * side, :],
            (((1,), (1,)), ((), ())),
            preferred_element_type=F32,
        )
        for at, j in enumerate(cols):
            row = blocks.index((i, j)) * side
            acc[row : row + side, :] += got[:, at * side : (at + 1) * side]

    @pl.when(step_id == pl.num_programs(0) - 1)
    def _():
        piece = out_ref.shape[1]
        for t, m in enumerate(order):
            rows = pl.multiple_of((me_ref[0] ^ m) * piece, math.gcd(piece, 8))
            out_ref[t] = acc[pl.ds(rows, piece), :] * gain


def run_margin(me, spreads, cells, side, order, blocks, after):
    parts, per, _, width = spreads[0].shape
    count = sum(s.shape[0] * s.shape[2] for s in spreads)
    size = len(blocks) * side
    shape = (parts, size // parts, side)
    return pl.pallas_call(
        functools.partial(
            margin_kernel, side=side, gain=1.0 / cells, order=order, blocks=blocks,
            sources=len(spreads),
        ),
        grid=(per,),
        in_specs=[pl.BlockSpec(memory_space=pltpu.SMEM)]
        + [pl.BlockSpec((parts, 1, s.shape[2], width), lambda x: (0, x, 0, 0)) for s in spreads]
        + [pl.BlockSpec(memory_space=pl.ANY)] * len(after),
        out_specs=pl.BlockSpec(shape, lambda x: (0, 0, 0)),
        out_shape=jax.ShapeDtypeStruct(shape, F32),
        scratch_shapes=[pltpu.VMEM((count, width), BF), pltpu.VMEM((size, side), F32)],
        compiler_params=pltpu.CompilerParams(vmem_limit_bytes=48 << 20),
        cost_estimate=pl.CostEstimate(
            flops=2 * size * side * width * per, bytes_accessed=2 * count * width * per,
            transcendentals=0,
        ),
        name="margin",
    )(me, *spreads, *after)


def stage_masks(parts):
    stages, low = [], 1
    while low < parts:
        bits = [low, 2 * low] if 2 * low < parts else [low]
        masks = [0]
        for b in bits:
            masks += [m ^ b for m in masks]
        stages.append(masks)
        low <<= len(bits)
    return stages


def piece_order(stages):
    order = [0]
    for masks in reversed(stages):
        order = [m ^ o for m in masks for o in order]
    return order


def send(value, mask, parts):
    return lax.ppermute(value, "orb", [(i, i ^ mask) for i in range(parts)])


def scatter_sum(held, stages, parts):
    for masks in stages:
        held = held.reshape((len(masks), -1) + held.shape[1:])
        total = held[0]
        for other in [send(held[i], m, parts) for i, m in enumerate(masks) if i]:
            total = total + other
        held = total
    return held


def gather_pieces(held, stages, parts):
    for masks in reversed(stages):
        got = [send(held, m, parts) for m in masks[1:]]
        held = jnp.concatenate([held] + got, axis=0)
    return held


def split(value):
    high = value.astype(BF)
    return high, (value - high.astype(F32)).astype(BF)


def mul(a, b):
    ah, al = a
    bh, bl = b
    dot = functools.partial(jnp.dot, preferred_element_type=F32)
    return dot(ah, bh) + (dot(ah, bl) + dot(al, bh))


def inverse_root_kernel(
    me_ref, held_ref, out_ref, packed, full, pval, zhi, zlo, *, masks, side, blocks, pieces
):
    me = me_ref[0]
    start = inner = 0
    for piece in pieces:
        for t, m in enumerate(masks):
            rows = pl.multiple_of(start + (me ^ m) * piece, math.gcd(piece, 8))
            packed[pl.ds(rows, piece), :] = held_ref[t, inner : inner + piece]
        start += piece * len(masks)
        inner += piece
    count = full.shape[0]
    for at, (i, j) in enumerate(blocks):
        tile = packed[at * side : (at + 1) * side, :]
        full[i * side : (i + 1) * side, j * side : (j + 1) * side] = tile
        if i != j:
            full[j * side : (j + 1) * side, i * side : (i + 1) * side] = tile.T
    margin = full[...]
    total = jnp.sum(jnp.sum(margin * margin, axis=1, keepdims=True), axis=0, keepdims=True)
    scale = jnp.sqrt(total + margin_eps)
    row = lax.broadcasted_iota(jnp.int32, (count, count), 0)
    col = lax.broadcasted_iota(jnp.int32, (count, count), 1)
    eye = jnp.where(row == col, 1.0, 0.0).astype(F32)

    def factor(ps, p):
        square = mul(ps, ps)
        inner = 6.75 * eye - 2.25 * p + 0.25 * square
        return 0.25 * (9.0 * eye - 9.75 * p + mul(split(square), split(inner)))

    def pair(p, last):
        ps = split(p)
        ws = split(factor(ps, p))
        return ws, None if last else mul(ws, split(mul(ws, ps)))

    ws, pval[...] = pair(margin / scale, False)
    zhi[...], zlo[...] = ws

    def middle(_, carry):
        ws, pval[...] = pair(pval[...], False)
        zhi[...], zlo[...] = split(mul(ws, (zhi[...], zlo[...])))
        return carry

    lax.fori_loop(0, ITERS // 2 - 2, middle, 0)
    ws, _ = pair(pval[...], True)
    z = mul(ws, (zhi[...], zlo[...]))
    out_ref[...] = (z / jnp.sqrt(scale)).astype(BF)


def run_inverse_root(me, held, masks, count, side, blocks, pieces):
    return pl.pallas_call(
        functools.partial(
            inverse_root_kernel, masks=masks, side=side, blocks=blocks, pieces=pieces
        ),
        in_specs=[
            pl.BlockSpec(memory_space=pltpu.SMEM),
            pl.BlockSpec(memory_space=pltpu.VMEM),
        ],
        out_specs=pl.BlockSpec(memory_space=pltpu.VMEM),
        out_shape=jax.ShapeDtypeStruct((count, count), BF),
        scratch_shapes=[
            pltpu.VMEM((len(blocks) * side, side), F32),
            pltpu.VMEM((count, count), F32),
            pltpu.VMEM((count, count), F32),
            pltpu.VMEM((count, count), BF),
            pltpu.VMEM((count, count), BF),
        ],
        compiler_params=pltpu.CompilerParams(vmem_limit_bytes=48 << 20),
        cost_estimate=pl.CostEstimate(
            flops=2 * 51 * count**3, bytes_accessed=4 * count * count, transcendentals=0
        ),
        name="inverse_root",
    )(me, held)


def rotate_kernel(*refs):
    coeff_ref, ins, out_ref, den_ref, flat = refs[0], refs[1:-3], refs[-3], refs[-2], refs[-1]
    parts, _, sets, group, width = out_ref.shape
    gather_rows(ins, flat)
    wide = jnp.dot(coeff_ref[...], flat[...], preferred_element_type=F32)
    wide = wide.astype(BF).astype(F32)
    for c in range(sets):
        own = wide[c * parts * group : (c + 1) * parts * group].reshape(parts, group, width)
        out_ref[:, 0, c] = own.astype(BF)
    den_ref[...] = jnp.sum(wide * wide, axis=0)[None, None]


def run_rotate(coeff, spreads):
    parts, per, group, width = spreads[0].shape
    own, count = coeff.shape
    sets = own // (parts * group)
    return pl.pallas_call(
        rotate_kernel,
        grid=(per,),
        in_specs=[full_spec(coeff)]
        + [pl.BlockSpec((parts, 1, s.shape[2], width), lambda x: (0, x, 0, 0)) for s in spreads],
        out_specs=[
            pl.BlockSpec((parts, 1, sets, group, width), lambda x: (0, x, 0, 0, 0)),
            pl.BlockSpec((1, 1, width), lambda x: (x, 0, 0)),
        ],
        out_shape=[
            jax.ShapeDtypeStruct((parts, per, sets, group, width), BF),
            jax.ShapeDtypeStruct((per, 1, width), F32),
        ],
        scratch_shapes=[pltpu.VMEM((count, width), BF)],
        compiler_params=pltpu.CompilerParams(vmem_limit_bytes=48 << 20),
        cost_estimate=pl.CostEstimate(
            flops=2 * count * own * width * per,
            bytes_accessed=2 * (count + own) * width * per,
            transcendentals=0,
        ),
        name="rotate",
    )(coeff, *spreads)


def restore_kernel(*refs):
    in_ref, out_ref = refs[0], refs[-1]
    parts, per, sets, group, lanes = in_ref.shape
    wide = in_ref[...].astype(F32).reshape(parts * per, sets * group, lanes)
    out_ref[...] = jnp.swapaxes(wide, 0, 1).astype(BF)


def run_restore(spread, target, chunk, chunks):
    parts, per, sets, group, width = spread.shape
    own, size_x = sets * group, parts * per
    args = (spread,) if target is None else (spread, target)
    return pl.pallas_call(
        restore_kernel,
        grid=(width // COLS,),
        in_specs=[pl.BlockSpec((parts, per, sets, group, COLS), lambda l: (0, 0, 0, 0, l))]
        + [pl.BlockSpec(memory_space=pl.ANY)] * (len(args) - 1),
        out_specs=pl.BlockSpec((own, size_x, COLS), lambda l: (chunk, 0, l)),
        out_shape=jax.ShapeDtypeStruct((own * chunks, size_x, width), BF),
        input_output_aliases={} if target is None else {1: 0},
        cost_estimate=pl.CostEstimate(
            flops=0, bytes_accessed=4 * own * size_x * width, transcendentals=0
        ),
        name="restore",
    )(*args)


def shards(orbitals, potential):
    parts = lax.axis_size("orb")
    mine, size_x, width = orbitals.shape[1:]
    chunks = max(1, mine // 8)
    outs = min(chunks, OUT_CHUNKS)
    count = mine * parts
    exchange = lambda v: lax.all_to_all(v, "orb", split_axis=0, concat_axis=0, tiled=True)
    me = lax.axis_index("orb").astype(jnp.int32).reshape(1)
    stages = stage_masks(parts)
    order = piece_order(stages)
    spreads = [
        exchange(run_filter(orbitals[0], c, chunks, potential, parts, 512))
        for c in range(chunks)
    ]
    early = (chunks - 1) * (count // chunks)
    blocks = triangle(early, LANES)
    last = [pair for pair in triangle(count, LANES) if pair not in blocks]
    helds = []
    for some, ready in ((blocks, spreads[:-1]), (last, spreads)):
        if some:
            partial = run_margin(me, ready, size_x * width, LANES, order, some, helds)
            helds.append(scatter_sum(partial, stages, parts))
    held = gather_pieces(jnp.concatenate(helds, axis=1), stages, parts)
    pieces = [h.shape[1] for h in helds]
    coeff = run_inverse_root(me, held, order, count, LANES, blocks + last, pieces)
    own = count // outs
    target = None
    density = 0.0
    returned = []
    for c in range(outs):
        rotated, part = run_rotate(coeff[c * own : (c + 1) * own], spreads)
        returned.append(exchange(rotated))
        density = density + part[:, 0]
    for c in range(outs):
        target = run_restore(returned[c], target, c, outs)
    kpoints = lax.axis_size("kpt")
    total = density
    for k in range(1, kpoints):
        total = total + lax.ppermute(
            density, "kpt", [(i, (i + k) % kpoints) for i in range(kpoints)]
        )
    weight = 1.0 / (kpoints * math.sqrt(count))
    return target[None], total * weight


def solution(mesh):
    in_specs = (P("kpt", "orb", None, None), P())
    out_specs = (P("kpt", "orb", None, None), P("orb", None))
    return jax.shard_map(shards, mesh=mesh, in_specs=in_specs, out_specs=out_specs, check_vma=False)
```

```python
import functools
import math

import jax
import jax.numpy as jnp
import numpy as np
from jax import lax
from jax.experimental import pallas as pl
from jax.experimental.pallas import tpu as pltpu
from jax.sharding import PartitionSpec as P

DEG = 4
ITERS = 8
LANES = 128
COLS = 256
OUT_CHUNKS = 2
BF = jnp.bfloat16
F32 = jnp.float32

filter_centre = 13.0
filter_half = 9.0
margin_eps = 1e-06


def circulant(taps, first, length):
    matrix = np.zeros((length, length))
    for k in range(len(taps)):
        for i in range(length):
            matrix[i, (i + first + k) % length] += taps[k]
    return matrix


def build_tables(size_x, width):
    side = math.isqrt(width)
    kinetic = [math.pi**2 / 6.0 if k == 0 else (-1.0) ** k / (k * k) for k in range(-14, 15)]
    taps = np.array([math.exp(-((k + 0.5) ** 2) / 6.0) for k in range(-8, 8)])
    taps = taps / taps.sum()
    kin_side = circulant(kinetic, -14, side)
    mag_side = circulant(taps, -8, side)
    kin_yz = np.kron(kin_side, np.eye(side)) + np.kron(np.eye(side), kin_side)
    mag_yz = np.kron(mag_side, mag_side)
    return circulant(kinetic, -14, size_x), circulant(taps, -8, size_x), kin_yz, mag_yz


def to_bf16(table):
    return jnp.asarray(np.asarray(table, np.float32)).astype(BF)


def full_spec(array):
    return pl.BlockSpec(array.shape, lambda *_: (0,) * array.ndim)


def filter_kernel(
    in_ref, pot_ref, kx_ref, mx_ref, kyz_ref, myz_ref, myzt_ref, out_ref,
    now, prev, smooth, mixed, back, nxt, fin, mxt_ref, *, first, firstt,
):
    size_x, width = in_ref.shape[1:]
    rows = now.shape[0]
    group = fin.shape[0] // size_x
    step_id = pl.program_id(0)
    blocks = width // COLS
    span = kx_ref.shape[0]
    tiles = [
        (slice(r, r + span), slice(c, c + COLS))
        for c in range(0, width, COLS)
        for r in range(0, rows, span)
    ]
    dot = functools.partial(jnp.dot, preferred_element_type=F32)
    mxt_ref[...] = mx_ref[...].astype(F32).T.astype(BF)
    start = in_ref[...].reshape(rows, width)
    now[:, :width] = start
    now[:, width:] = start
    prev[...] = start

    def window(src, table, n, lead):
        at = (n + lead) % blocks * COLS
        return dot(src[:, at : at + table.shape[0]], table[...])

    def step(j, carry):
        gain = jnp.where(j == 0, 1.0 / filter_half, 2.0 / filter_half).astype(F32)
        keep = jnp.where(j == 0, 0.0, 1.0).astype(F32)
        for n in range(blocks):
            smooth[:, n * COLS : (n + 1) * COLS] = window(now, myz_ref, n, first).astype(BF)
        for rs, cs in tiles:
            value = dot(mx_ref[...], smooth[rs, cs])
            value = value.reshape(span // size_x, size_x, COLS) * pot_ref[:, cs][None]
            mixed[rs, cs] = value.reshape(span, COLS).astype(BF)
        for rs, cs in tiles:
            value = dot(mxt_ref[...], mixed[rs, cs]).astype(BF)
            back[rs, cs] = value
            back[rs, cs.start + width : cs.stop + width] = value
        for n in range(blocks):
            cs = slice(n * COLS, (n + 1) * COLS)
            total = window(now, kyz_ref, n, 0) + window(back, myzt_ref, n, firstt)
            for r in range(0, rows, span):
                rs = slice(r, r + span)
                value = now[rs, cs]
                shifted = total[rs] + dot(kx_ref[...], value) - filter_centre * value.astype(F32)
                nxt[rs, cs] = (gain * shifted - keep * prev[rs, cs].astype(F32)).astype(BF)
        prev[...] = now[:, :width]
        now[:, :width] = nxt[...]
        now[:, width:] = nxt[...]
        return carry

    lax.fori_loop(0, DEG, step, 0)
    fin[pl.ds(pl.multiple_of(step_id * rows, rows), rows), :] = nxt[...]

    @pl.when(step_id == pl.num_programs(0) - 1)
    def _():
        turned = jnp.swapaxes(fin[...].reshape(group, size_x, width), 0, 1)
        out_ref[...] = turned.reshape(out_ref.shape)


def run_filter(orbitals, chunk, chunks, potential, parts, rows):
    size_x, width = orbitals.shape[1:]
    group = orbitals.shape[0] // chunks
    rows = min(rows, group * size_x)
    blocks = width // COLS
    kin_x, mag_x, kin_yz, mag_yz = build_tables(size_x, width)
    span = min(256, rows)
    wide = lambda t: to_bf16(np.kron(np.eye(span // size_x), t))
    piece = lambda t, d: t[:COLS, d % blocks * COLS : (d % blocks + 1) * COLS].T

    def band(t):
        used = [d for d in range(blocks) if np.any(piece(t, d))]
        lead = [d for d in used if (d - 1) % blocks not in used]
        lead = lead[0] if lead else 0
        return lead, to_bf16(np.concatenate([piece(t, lead + i) for i in range(len(used))], 0))

    _, kyz = band(kin_yz)
    first, myz = band(mag_yz)
    firstt, myzt = band(mag_yz.T)
    args = (orbitals, potential, wide(kin_x), wide(mag_x), kyz, myz, myzt)
    per = size_x // parts
    steps = group * size_x // rows
    return pl.pallas_call(
        functools.partial(filter_kernel, first=first, firstt=firstt),
        grid=(steps,),
        in_specs=[
            pl.BlockSpec((rows // size_x, size_x, width), lambda s: (chunk * steps + s, 0, 0))
        ]
        + [full_spec(a) for a in args[1:]],
        out_specs=pl.BlockSpec((parts, per, group, width), lambda s: (0, 0, 0, 0)),
        out_shape=jax.ShapeDtypeStruct((parts, per, group, width), BF),
        scratch_shapes=[
            pltpu.VMEM((rows, 2 * width), BF),
            pltpu.VMEM((rows, width), BF),
            pltpu.VMEM((rows, width), BF),
            pltpu.VMEM((rows, width), BF),
            pltpu.VMEM((rows, 2 * width), BF),
            pltpu.VMEM((rows, width), BF),
            pltpu.VMEM((group * size_x, width), BF),
            pltpu.VMEM((span, span), BF),
        ],
        compiler_params=pltpu.CompilerParams(vmem_limit_bytes=56 << 20),
        cost_estimate=pl.CostEstimate(
            flops=2 * DEG * group * size_x * width
            * (kyz.shape[0] + myz.shape[0] + myzt.shape[0] + 3 * span),
            bytes_accessed=4 * group * size_x * width,
            transcendentals=0,
        ),
        name="chebyshev",
    )(*args)


def triangle(count, side):
    n = count // side
    return [(i, j) for i in range(n) for j in range(i, n)]


def gather_rows(ins, flat):
    start = 0
    for ref in ins:
        size = ref.shape[0] * ref.shape[2]
        flat[start : start + size, :] = (
            ref[:, 0].astype(F32).reshape(size, flat.shape[1]).astype(BF)
        )
        start += size


def margin_kernel(me_ref, *refs, side, gain, order, blocks, sources):
    ins, out_ref, flat, acc = refs[:sources], refs[-3], refs[-2], refs[-1]
    step_id = pl.program_id(0)
    gather_rows(ins, flat)

    @pl.when(step_id == 0)
    def _():
        acc[...] = jnp.zeros_like(acc)

    for i in sorted({i for i, _ in blocks}):
        cols = [j for b, j in blocks if b == i]
        got = lax.dot_general(
            flat[i * side : (i + 1) * side, :],
            flat[cols[0] * side : (cols[-1] + 1) * side, :],
            (((1,), (1,)), ((), ())),
            preferred_element_type=F32,
        )
        for at, j in enumerate(cols):
            row = blocks.index((i, j)) * side
            acc[row : row + side, :] += got[:, at * side : (at + 1) * side]

    @pl.when(step_id == pl.num_programs(0) - 1)
    def _():
        piece = out_ref.shape[1]
        for t, m in enumerate(order):
            rows = pl.multiple_of((me_ref[0] ^ m) * piece, math.gcd(piece, 8))
            out_ref[t] = acc[pl.ds(rows, piece), :] * gain


def run_margin(me, spreads, cells, side, order, blocks, after):
    parts, per, _, width = spreads[0].shape
    count = sum(s.shape[0] * s.shape[2] for s in spreads)
    size = len(blocks) * side
    shape = (parts, size // parts, side)
    return pl.pallas_call(
        functools.partial(
            margin_kernel, side=side, gain=1.0 / cells, order=order, blocks=blocks,
            sources=len(spreads),
        ),
        grid=(per,),
        in_specs=[pl.BlockSpec(memory_space=pltpu.SMEM)]
        + [pl.BlockSpec((parts, 1, s.shape[2], width), lambda x: (0, x, 0, 0)) for s in spreads]
        + [pl.BlockSpec(memory_space=pl.ANY)] * len(after),
        out_specs=pl.BlockSpec(shape, lambda x: (0, 0, 0)),
        out_shape=jax.ShapeDtypeStruct(shape, F32),
        scratch_shapes=[pltpu.VMEM((count, width), BF), pltpu.VMEM((size, side), F32)],
        compiler_params=pltpu.CompilerParams(vmem_limit_bytes=48 << 20),
        cost_estimate=pl.CostEstimate(
            flops=2 * size * side * width * per, bytes_accessed=2 * count * width * per,
            transcendentals=0,
        ),
        name="margin",
    )(me, *spreads, *after)


def stage_masks(parts):
    stages, low = [], 1
    while low < parts:
        bits = [low, 2 * low] if 2 * low < parts else [low]
        masks = [0]
        for b in bits:
            masks += [m ^ b for m in masks]
        stages.append(masks)
        low <<= len(bits)
    return stages


def piece_order(stages):
    order = [0]
    for masks in reversed(stages):
        order = [m ^ o for m in masks for o in order]
    return order


def send(value, mask, parts):
    return lax.ppermute(value, "orb", [(i, i ^ mask) for i in range(parts)])


def scatter_sum(held, stages, parts):
    for masks in stages:
        held = held.reshape((len(masks), -1) + held.shape[1:])
        total = held[0]
        for other in [send(held[i], m, parts) for i, m in enumerate(masks) if i]:
            total = total + other
        held = total
    return held


def gather_pieces(held, stages, parts):
    for masks in reversed(stages):
        got = [send(held, m, parts) for m in masks[1:]]
        held = jnp.concatenate([held] + got, axis=0)
    return held


def split(value):
    high = value.astype(BF)
    return high, (value - high.astype(F32)).astype(BF)


def mul(a, b):
    ah, al = a
    bh, bl = b
    dot = functools.partial(jnp.dot, preferred_element_type=F32)
    return dot(ah, bh) + (dot(ah, bl) + dot(al, bh))


def inverse_root_kernel(
    me_ref, held_ref, out_ref, packed, full, pval, zhi, zlo, *, masks, side, blocks, pieces
):
    me = me_ref[0]
    start = inner = 0
    for piece in pieces:
        for t, m in enumerate(masks):
            rows = pl.multiple_of(start + (me ^ m) * piece, math.gcd(piece, 8))
            packed[pl.ds(rows, piece), :] = held_ref[t, inner : inner + piece]
        start += piece * len(masks)
        inner += piece
    count = full.shape[0]
    for at, (i, j) in enumerate(blocks):
        tile = packed[at * side : (at + 1) * side, :]
        full[i * side : (i + 1) * side, j * side : (j + 1) * side] = tile
        if i != j:
            full[j * side : (j + 1) * side, i * side : (i + 1) * side] = tile.T
    margin = full[...]
    total = jnp.sum(jnp.sum(margin * margin, axis=1, keepdims=True), axis=0, keepdims=True)
    scale = jnp.sqrt(total + margin_eps)
    row = lax.broadcasted_iota(jnp.int32, (count, count), 0)
    col = lax.broadcasted_iota(jnp.int32, (count, count), 1)
    eye = jnp.where(row == col, 1.0, 0.0).astype(F32)

    def factor(ps, p):
        square = mul(ps, ps)
        inner = 6.75 * eye - 2.25 * p + 0.25 * square
        return 0.25 * (9.0 * eye - 9.75 * p + mul(split(square), split(inner)))

    def pair(p, last):
        ps = split(p)
        ws = split(factor(ps, p))
        return ws, None if last else mul(ws, split(mul(ws, ps)))

    ws, pval[...] = pair(margin / scale, False)
    zhi[...], zlo[...] = ws

    def middle(_, carry):
        ws, pval[...] = pair(pval[...], False)
        zhi[...], zlo[...] = split(mul(ws, (zhi[...], zlo[...])))
        return carry

    lax.fori_loop(0, ITERS // 2 - 2, middle, 0)
    ws, _ = pair(pval[...], True)
    z = mul(ws, (zhi[...], zlo[...]))
    out_ref[...] = (z / jnp.sqrt(scale)).astype(BF)


def run_inverse_root(me, held, masks, count, side, blocks, pieces):
    return pl.pallas_call(
        functools.partial(
            inverse_root_kernel, masks=masks, side=side, blocks=blocks, pieces=pieces
        ),
        in_specs=[
            pl.BlockSpec(memory_space=pltpu.SMEM),
            pl.BlockSpec(memory_space=pltpu.VMEM),
        ],
        out_specs=pl.BlockSpec(memory_space=pltpu.VMEM),
        out_shape=jax.ShapeDtypeStruct((count, count), BF),
        scratch_shapes=[
            pltpu.VMEM((len(blocks) * side, side), F32),
            pltpu.VMEM((count, count), F32),
            pltpu.VMEM((count, count), F32),
            pltpu.VMEM((count, count), BF),
            pltpu.VMEM((count, count), BF),
        ],
        compiler_params=pltpu.CompilerParams(vmem_limit_bytes=48 << 20),
        cost_estimate=pl.CostEstimate(
            flops=2 * 51 * count**3, bytes_accessed=4 * count * count, transcendentals=0
        ),
        name="inverse_root",
    )(me, held)


def rotate_kernel(*refs):
    coeff_ref, ins, out_ref, den_ref, flat = refs[0], refs[1:-3], refs[-3], refs[-2], refs[-1]
    parts, _, sets, group, width = out_ref.shape
    gather_rows(ins, flat)
    wide = jnp.dot(coeff_ref[...], flat[...], preferred_element_type=F32)
    wide = wide.astype(BF).astype(F32)
    for c in range(sets):
        own = wide[c * parts * group : (c + 1) * parts * group].reshape(parts, group, width)
        out_ref[:, 0, c] = own.astype(BF)
    den_ref[...] = jnp.sum(wide * wide, axis=0)[None, None]


def run_rotate(coeff, spreads):
    parts, per, group, width = spreads[0].shape
    own, count = coeff.shape
    sets = own // (parts * group)
    return pl.pallas_call(
        rotate_kernel,
        grid=(per,),
        in_specs=[full_spec(coeff)]
        + [pl.BlockSpec((parts, 1, s.shape[2], width), lambda x: (0, x, 0, 0)) for s in spreads],
        out_specs=[
            pl.BlockSpec((parts, 1, sets, group, width), lambda x: (0, x, 0, 0, 0)),
            pl.BlockSpec((1, 1, width), lambda x: (x, 0, 0)),
        ],
        out_shape=[
            jax.ShapeDtypeStruct((parts, per, sets, group, width), BF),
            jax.ShapeDtypeStruct((per, 1, width), F32),
        ],
        scratch_shapes=[pltpu.VMEM((count, width), BF)],
        compiler_params=pltpu.CompilerParams(vmem_limit_bytes=48 << 20),
        cost_estimate=pl.CostEstimate(
            flops=2 * count * own * width * per,
            bytes_accessed=2 * (count + own) * width * per,
            transcendentals=0,
        ),
        name="rotate",
    )(coeff, *spreads)


def restore_kernel(*refs):
    in_ref, out_ref = refs[0], refs[-1]
    _, per, sets, group, width = in_ref.shape
    some = out_ref.shape[1] // per
    first = pl.multiple_of(pl.program_id(0) * some, some)
    wide = in_ref[pl.ds(first, some)].astype(F32).reshape(some * per, sets * group, width)
    out_ref[...] = jnp.swapaxes(wide, 0, 1).astype(BF)


def run_restore(spread, target, chunk, chunks):
    parts, per, sets, group, width = spread.shape
    own, size_x = sets * group, parts * per
    rows = max(16, per)
    args = (spread,) if target is None else (spread, target)
    return pl.pallas_call(
        restore_kernel,
        grid=(size_x // rows,),
        in_specs=[pl.BlockSpec(memory_space=pltpu.VMEM)]
        + [pl.BlockSpec(memory_space=pl.ANY)] * (len(args) - 1),
        out_specs=pl.BlockSpec((own, rows, width), lambda x: (chunk, x, 0)),
        out_shape=jax.ShapeDtypeStruct((own * chunks, size_x, width), BF),
        input_output_aliases={} if target is None else {1: 0},
        compiler_params=pltpu.CompilerParams(vmem_limit_bytes=48 << 20),
        cost_estimate=pl.CostEstimate(
            flops=0, bytes_accessed=4 * own * size_x * width, transcendentals=0
        ),
        name="restore",
    )(*args)


def shards(orbitals, potential):
    parts = lax.axis_size("orb")
    mine, size_x, width = orbitals.shape[1:]
    chunks = max(1, mine // 8)
    outs = min(chunks, OUT_CHUNKS)
    count = mine * parts
    exchange = lambda v: lax.all_to_all(v, "orb", split_axis=0, concat_axis=0, tiled=True)
    me = lax.axis_index("orb").astype(jnp.int32).reshape(1)
    stages = stage_masks(parts)
    order = piece_order(stages)
    spreads = [
        exchange(run_filter(orbitals[0], c, chunks, potential, parts, 512))
        for c in range(chunks)
    ]
    early = (chunks - 1) * (count // chunks)
    blocks = triangle(early, LANES)
    last = [pair for pair in triangle(count, LANES) if pair not in blocks]
    helds = []
    for some, ready in ((blocks, spreads[:-1]), (last, spreads)):
        if some:
            partial = run_margin(me, ready, size_x * width, LANES, order, some, helds)
            helds.append(scatter_sum(partial, stages[:1], parts))
    held = scatter_sum(jnp.concatenate(helds, axis=1), stages[1:], parts)
    held = gather_pieces(held, stages, parts)
    pieces = [h.shape[1] for h in helds]
    coeff = run_inverse_root(me, held, order, count, LANES, blocks + last, pieces)
    own = count // outs
    target = None
    density = 0.0
    returned = []
    for c in range(outs):
        rotated, part = run_rotate(coeff[c * own : (c + 1) * own], spreads)
        returned.append(exchange(rotated))
        density = density + part[:, 0]
    for c in range(outs):
        target = run_restore(returned[c], target, c, outs)
    kpoints = lax.axis_size("kpt")
    total = density
    for k in range(1, kpoints):
        total = total + lax.ppermute(
            density, "kpt", [(i, (i + k) % kpoints) for i in range(kpoints)]
        )
    weight = 1.0 / (kpoints * math.sqrt(count))
    return target[None], total * weight


def solution(mesh):
    in_specs = (P("kpt", "orb", None, None), P())
    out_specs = (P("kpt", "orb", None, None), P("orb", None))
    return jax.shard_map(shards, mesh=mesh, in_specs=in_specs, out_specs=out_specs, check_vma=False)
```

```python
import functools
import math

import jax
import jax.numpy as jnp
import numpy as np
from jax import lax
from jax.experimental import pallas as pl
from jax.experimental.pallas import tpu as pltpu
from jax.sharding import PartitionSpec as P

DEG = 4
ITERS = 8
LANES = 128
COLS = 256
OUT_CHUNKS = 1
BF = jnp.bfloat16
F32 = jnp.float32

filter_centre = 13.0
filter_half = 9.0
margin_eps = 1e-06


def circulant(taps, first, length):
    matrix = np.zeros((length, length))
    for k in range(len(taps)):
        for i in range(length):
            matrix[i, (i + first + k) % length] += taps[k]
    return matrix


def build_tables(size_x, width):
    side = math.isqrt(width)
    kinetic = [math.pi**2 / 6.0 if k == 0 else (-1.0) ** k / (k * k) for k in range(-14, 15)]
    taps = np.array([math.exp(-((k + 0.5) ** 2) / 6.0) for k in range(-8, 8)])
    taps = taps / taps.sum()
    kin_side = circulant(kinetic, -14, side)
    mag_side = circulant(taps, -8, side)
    kin_yz = np.kron(kin_side, np.eye(side)) + np.kron(np.eye(side), kin_side)
    mag_yz = np.kron(mag_side, mag_side)
    return circulant(kinetic, -14, size_x), circulant(taps, -8, size_x), kin_yz, mag_yz


def to_bf16(table):
    return jnp.asarray(np.asarray(table, np.float32)).astype(BF)


def full_spec(array):
    return pl.BlockSpec(array.shape, lambda *_: (0,) * array.ndim)


def filter_kernel(
    in_ref, pot_ref, kx_ref, mx_ref, kyz_ref, myz_ref, myzt_ref, out_ref,
    now, prev, smooth, mixed, back, nxt, fin, mxt_ref, *, first, firstt,
):
    size_x, width = in_ref.shape[1:]
    rows = now.shape[0]
    group = fin.shape[0] // size_x
    step_id = pl.program_id(0)
    blocks = width // COLS
    span = kx_ref.shape[0]
    tiles = [
        (slice(r, r + span), slice(c, c + COLS))
        for c in range(0, width, COLS)
        for r in range(0, rows, span)
    ]
    dot = functools.partial(jnp.dot, preferred_element_type=F32)
    mxt_ref[...] = mx_ref[...].astype(F32).T.astype(BF)
    start = in_ref[...].reshape(rows, width)
    now[:, :width] = start
    now[:, width:] = start
    prev[...] = start

    def window(src, table, n, lead):
        at = (n + lead) % blocks * COLS
        return dot(src[:, at : at + table.shape[0]], table[...])

    def step(j, carry):
        gain = jnp.where(j == 0, 1.0 / filter_half, 2.0 / filter_half).astype(F32)
        keep = jnp.where(j == 0, 0.0, 1.0).astype(F32)
        for n in range(blocks):
            smooth[:, n * COLS : (n + 1) * COLS] = window(now, myz_ref, n, first).astype(BF)
        for rs, cs in tiles:
            value = dot(mx_ref[...], smooth[rs, cs])
            value = value.reshape(span // size_x, size_x, COLS) * pot_ref[:, cs][None]
            mixed[rs, cs] = value.reshape(span, COLS).astype(BF)
        for rs, cs in tiles:
            value = dot(mxt_ref[...], mixed[rs, cs]).astype(BF)
            back[rs, cs] = value
            back[rs, cs.start + width : cs.stop + width] = value
        for n in range(blocks):
            cs = slice(n * COLS, (n + 1) * COLS)
            total = window(now, kyz_ref, n, 0) + window(back, myzt_ref, n, firstt)
            for r in range(0, rows, span):
                rs = slice(r, r + span)
                value = now[rs, cs]
                shifted = total[rs] + dot(kx_ref[...], value) - filter_centre * value.astype(F32)
                nxt[rs, cs] = (gain * shifted - keep * prev[rs, cs].astype(F32)).astype(BF)
        prev[...] = now[:, :width]
        now[:, :width] = nxt[...]
        now[:, width:] = nxt[...]
        return carry

    lax.fori_loop(0, DEG, step, 0)
    fin[pl.ds(pl.multiple_of(step_id * rows, rows), rows), :] = nxt[...]

    @pl.when(step_id == pl.num_programs(0) - 1)
    def _():
        turned = jnp.swapaxes(fin[...].reshape(group, size_x, width), 0, 1)
        out_ref[...] = turned.reshape(out_ref.shape)


def run_filter(orbitals, chunk, chunks, potential, parts, rows):
    size_x, width = orbitals.shape[1:]
    group = orbitals.shape[0] // chunks
    rows = min(rows, group * size_x)
    blocks = width // COLS
    kin_x, mag_x, kin_yz, mag_yz = build_tables(size_x, width)
    span = min(256, rows)
    wide = lambda t: to_bf16(np.kron(np.eye(span // size_x), t))
    piece = lambda t, d: t[:COLS, d % blocks * COLS : (d % blocks + 1) * COLS].T

    def band(t):
        used = [d for d in range(blocks) if np.any(piece(t, d))]
        lead = [d for d in used if (d - 1) % blocks not in used]
        lead = lead[0] if lead else 0
        return lead, to_bf16(np.concatenate([piece(t, lead + i) for i in range(len(used))], 0))

    _, kyz = band(kin_yz)
    first, myz = band(mag_yz)
    firstt, myzt = band(mag_yz.T)
    args = (orbitals, potential, wide(kin_x), wide(mag_x), kyz, myz, myzt)
    per = size_x // parts
    steps = group * size_x // rows
    return pl.pallas_call(
        functools.partial(filter_kernel, first=first, firstt=firstt),
        grid=(steps,),
        in_specs=[
            pl.BlockSpec((rows // size_x, size_x, width), lambda s: (chunk * steps + s, 0, 0))
        ]
        + [full_spec(a) for a in args[1:]],
        out_specs=pl.BlockSpec((parts, per, group, width), lambda s: (0, 0, 0, 0)),
        out_shape=jax.ShapeDtypeStruct((parts, per, group, width), BF),
        scratch_shapes=[
            pltpu.VMEM((rows, 2 * width), BF),
            pltpu.VMEM((rows, width), BF),
            pltpu.VMEM((rows, width), BF),
            pltpu.VMEM((rows, width), BF),
            pltpu.VMEM((rows, 2 * width), BF),
            pltpu.VMEM((rows, width), BF),
            pltpu.VMEM((group * size_x, width), BF),
            pltpu.VMEM((span, span), BF),
        ],
        compiler_params=pltpu.CompilerParams(vmem_limit_bytes=56 << 20),
        cost_estimate=pl.CostEstimate(
            flops=2 * DEG * group * size_x * width
            * (kyz.shape[0] + myz.shape[0] + myzt.shape[0] + 3 * span),
            bytes_accessed=4 * group * size_x * width,
            transcendentals=0,
        ),
        name="chebyshev",
    )(*args)


def triangle(count, side):
    n = count // side
    return [(i, j) for i in range(n) for j in range(i, n)]


def gather_rows(ins, flat):
    start = 0
    for ref in ins:
        size = ref.shape[0] * ref.shape[2]
        flat[start : start + size, :] = (
            ref[:, 0].astype(F32).reshape(size, flat.shape[1]).astype(BF)
        )
        start += size


def margin_kernel(me_ref, *refs, side, gain, order, blocks, sources):
    ins, out_ref, flat, acc = refs[:sources], refs[-3], refs[-2], refs[-1]
    step_id = pl.program_id(0)
    gather_rows(ins, flat)

    @pl.when(step_id == 0)
    def _():
        acc[...] = jnp.zeros_like(acc)

    for i in sorted({i for i, _ in blocks}):
        cols = [j for b, j in blocks if b == i]
        got = lax.dot_general(
            flat[i * side : (i + 1) * side, :],
            flat[cols[0] * side : (cols[-1] + 1) * side, :],
            (((1,), (1,)), ((), ())),
            preferred_element_type=F32,
        )
        for at, j in enumerate(cols):
            row = blocks.index((i, j)) * side
            acc[row : row + side, :] += got[:, at * side : (at + 1) * side]

    @pl.when(step_id == pl.num_programs(0) - 1)
    def _():
        piece = out_ref.shape[1]
        for t, m in enumerate(order):
            rows = pl.multiple_of((me_ref[0] ^ m) * piece, math.gcd(piece, 8))
            out_ref[t] = acc[pl.ds(rows, piece), :] * gain


def run_margin(me, spreads, cells, side, order, blocks, after):
    parts, per, _, width = spreads[0].shape
    count = sum(s.shape[0] * s.shape[2] for s in spreads)
    size = len(blocks) * side
    shape = (parts, size // parts, side)
    return pl.pallas_call(
        functools.partial(
            margin_kernel, side=side, gain=1.0 / cells, order=order, blocks=blocks,
            sources=len(spreads),
        ),
        grid=(per,),
        in_specs=[pl.BlockSpec(memory_space=pltpu.SMEM)]
        + [pl.BlockSpec((parts, 1, s.shape[2], width), lambda x: (0, x, 0, 0)) for s in spreads]
        + [pl.BlockSpec(memory_space=pl.ANY)] * len(after),
        out_specs=pl.BlockSpec(shape, lambda x: (0, 0, 0)),
        out_shape=jax.ShapeDtypeStruct(shape, F32),
        scratch_shapes=[pltpu.VMEM((count, width), BF), pltpu.VMEM((size, side), F32)],
        compiler_params=pltpu.CompilerParams(vmem_limit_bytes=48 << 20),
        cost_estimate=pl.CostEstimate(
            flops=2 * size * side * width * per, bytes_accessed=2 * count * width * per,
            transcendentals=0,
        ),
        name="margin",
    )(me, *spreads, *after)


def stage_masks(parts):
    stages, low = [], 1
    while low < parts:
        bits = [low, 2 * low] if 2 * low < parts else [low]
        masks = [0]
        for b in bits:
            masks += [m ^ b for m in masks]
        stages.append(masks)
        low <<= len(bits)
    return stages


def piece_order(stages):
    order = [0]
    for masks in reversed(stages):
        order = [m ^ o for m in masks for o in order]
    return order


def send(value, mask, parts):
    return lax.ppermute(value, "orb", [(i, i ^ mask) for i in range(parts)])


def scatter_sum(held, stages, parts):
    for masks in stages:
        held = held.reshape((len(masks), -1) + held.shape[1:])
        total = held[0]
        for other in [send(held[i], m, parts) for i, m in enumerate(masks) if i]:
            total = total + other
        held = total
    return held


def gather_pieces(held, stages, parts):
    for masks in reversed(stages):
        got = [send(held, m, parts) for m in masks[1:]]
        held = jnp.concatenate([held] + got, axis=0)
    return held


def split(value):
    high = value.astype(BF)
    return high, (value - high.astype(F32)).astype(BF)


def mul(a, b):
    ah, al = a
    bh, bl = b
    dot = functools.partial(jnp.dot, preferred_element_type=F32)
    return dot(ah, bh) + (dot(ah, bl) + dot(al, bh))


def inverse_root_kernel(
    me_ref, held_ref, out_ref, packed, full, pval, zhi, zlo, *, masks, side, blocks, pieces
):
    me = me_ref[0]
    start = inner = 0
    for piece in pieces:
        for t, m in enumerate(masks):
            rows = pl.multiple_of(start + (me ^ m) * piece, math.gcd(piece, 8))
            packed[pl.ds(rows, piece), :] = held_ref[t, inner : inner + piece]
        start += piece * len(masks)
        inner += piece
    count = full.shape[0]
    for at, (i, j) in enumerate(blocks):
        tile = packed[at * side : (at + 1) * side, :]
        full[i * side : (i + 1) * side, j * side : (j + 1) * side] = tile
        if i != j:
            full[j * side : (j + 1) * side, i * side : (i + 1) * side] = tile.T
    margin = full[...]
    total = jnp.sum(jnp.sum(margin * margin, axis=1, keepdims=True), axis=0, keepdims=True)
    scale = jnp.sqrt(total + margin_eps)
    row = lax.broadcasted_iota(jnp.int32, (count, count), 0)
    col = lax.broadcasted_iota(jnp.int32, (count, count), 1)
    eye = jnp.where(row == col, 1.0, 0.0).astype(F32)

    def factor(ps, p):
        square = mul(ps, ps)
        inner = 6.75 * eye - 2.25 * p + 0.25 * square
        return 0.25 * (9.0 * eye - 9.75 * p + mul(split(square), split(inner)))

    def pair(p, last):
        ps = split(p)
        ws = split(factor(ps, p))
        return ws, None if last else mul(ws, split(mul(ws, ps)))

    ws, pval[...] = pair(margin / scale, False)
    zhi[...], zlo[...] = ws

    def middle(_, carry):
        ws, pval[...] = pair(pval[...], False)
        zhi[...], zlo[...] = split(mul(ws, (zhi[...], zlo[...])))
        return carry

    lax.fori_loop(0, ITERS // 2 - 2, middle, 0)
    ws, _ = pair(pval[...], True)
    z = mul(ws, (zhi[...], zlo[...]))
    out_ref[...] = (z / jnp.sqrt(scale)).astype(BF)


def run_inverse_root(me, held, masks, count, side, blocks, pieces):
    return pl.pallas_call(
        functools.partial(
            inverse_root_kernel, masks=masks, side=side, blocks=blocks, pieces=pieces
        ),
        in_specs=[
            pl.BlockSpec(memory_space=pltpu.SMEM),
            pl.BlockSpec(memory_space=pltpu.VMEM),
        ],
        out_specs=pl.BlockSpec(memory_space=pltpu.VMEM),
        out_shape=jax.ShapeDtypeStruct((count, count), BF),
        scratch_shapes=[
            pltpu.VMEM((len(blocks) * side, side), F32),
            pltpu.VMEM((count, count), F32),
            pltpu.VMEM((count, count), F32),
            pltpu.VMEM((count, count), BF),
            pltpu.VMEM((count, count), BF),
        ],
        compiler_params=pltpu.CompilerParams(vmem_limit_bytes=48 << 20),
        cost_estimate=pl.CostEstimate(
            flops=2 * 51 * count**3, bytes_accessed=4 * count * count, transcendentals=0
        ),
        name="inverse_root",
    )(me, held)


def rotate_kernel(*refs):
    coeff_ref, ins, out_ref, den_ref, flat = refs[0], refs[1:-3], refs[-3], refs[-2], refs[-1]
    parts, _, sets, group, width = out_ref.shape
    gather_rows(ins, flat)
    wide = jnp.dot(coeff_ref[...], flat[...], preferred_element_type=F32)
    wide = wide.astype(BF).astype(F32)
    for c in range(sets):
        own = wide[c * parts * group : (c + 1) * parts * group].reshape(parts, group, width)
        out_ref[:, 0, c] = own.astype(BF)
    den_ref[...] = jnp.sum(wide * wide, axis=0)[None, None]


def run_rotate(coeff, spreads):
    parts, per, group, width = spreads[0].shape
    own, count = coeff.shape
    sets = own // (parts * group)
    return pl.pallas_call(
        rotate_kernel,
        grid=(per,),
        in_specs=[full_spec(coeff)]
        + [pl.BlockSpec((parts, 1, s.shape[2], width), lambda x: (0, x, 0, 0)) for s in spreads],
        out_specs=[
            pl.BlockSpec((parts, 1, sets, group, width), lambda x: (0, x, 0, 0, 0)),
            pl.BlockSpec((1, 1, width), lambda x: (x, 0, 0)),
        ],
        out_shape=[
            jax.ShapeDtypeStruct((parts, per, sets, group, width), BF),
            jax.ShapeDtypeStruct((per, 1, width), F32),
        ],
        scratch_shapes=[pltpu.VMEM((count, width), BF)],
        compiler_params=pltpu.CompilerParams(vmem_limit_bytes=48 << 20),
        cost_estimate=pl.CostEstimate(
            flops=2 * count * own * width * per,
            bytes_accessed=2 * (count + own) * width * per,
            transcendentals=0,
        ),
        name="rotate",
    )(coeff, *spreads)


def restore_kernel(*refs):
    in_ref, out_ref = refs[0], refs[-1]
    _, per, sets, group, width = in_ref.shape
    some = out_ref.shape[1] // per
    first = pl.multiple_of(pl.program_id(0) * some, some)
    wide = in_ref[pl.ds(first, some)].astype(F32).reshape(some * per, sets * group, width)
    out_ref[...] = jnp.swapaxes(wide, 0, 1).astype(BF)


def run_restore(spread, target, chunk, chunks):
    parts, per, sets, group, width = spread.shape
    own, size_x = sets * group, parts * per
    rows = max(16, per)
    args = (spread,) if target is None else (spread, target)
    return pl.pallas_call(
        restore_kernel,
        grid=(size_x // rows,),
        in_specs=[pl.BlockSpec(memory_space=pltpu.VMEM)]
        + [pl.BlockSpec(memory_space=pl.ANY)] * (len(args) - 1),
        out_specs=pl.BlockSpec((own, rows, width), lambda x: (chunk, x, 0)),
        out_shape=jax.ShapeDtypeStruct((own * chunks, size_x, width), BF),
        input_output_aliases={} if target is None else {1: 0},
        compiler_params=pltpu.CompilerParams(vmem_limit_bytes=48 << 20),
        cost_estimate=pl.CostEstimate(
            flops=0, bytes_accessed=4 * own * size_x * width, transcendentals=0
        ),
        name="restore",
    )(*args)


def shards(orbitals, potential):
    parts = lax.axis_size("orb")
    mine, size_x, width = orbitals.shape[1:]
    chunks = max(1, mine // 8)
    outs = min(chunks, OUT_CHUNKS)
    count = mine * parts
    exchange = lambda v: lax.all_to_all(v, "orb", split_axis=0, concat_axis=0, tiled=True)
    me = lax.axis_index("orb").astype(jnp.int32).reshape(1)
    stages = stage_masks(parts)
    order = piece_order(stages)
    spreads = [
        exchange(run_filter(orbitals[0], c, chunks, potential, parts, 512))
        for c in range(chunks)
    ]
    early = (chunks - 1) * (count // chunks)
    blocks = triangle(early, LANES)
    last = [pair for pair in triangle(count, LANES) if pair not in blocks]
    helds = []
    for some, ready in ((blocks, spreads[:-1]), (last, spreads)):
        if some:
            partial = run_margin(me, ready, size_x * width, LANES, order, some, helds)
            helds.append(scatter_sum(partial, stages[:1], parts))
    held = scatter_sum(jnp.concatenate(helds, axis=1), stages[1:], parts)
    held = gather_pieces(held, stages, parts)
    pieces = [h.shape[1] for h in helds]
    coeff = run_inverse_root(me, held, order, count, LANES, blocks + last, pieces)
    own = count // outs
    target = None
    density = 0.0
    returned = []
    for c in range(outs):
        rotated, part = run_rotate(coeff[c * own : (c + 1) * own], spreads)
        returned.append(exchange(rotated))
        density = density + part[:, 0]
    for c in range(outs):
        target = run_restore(returned[c], target, c, outs)
    kpoints = lax.axis_size("kpt")
    total = density
    for k in range(1, kpoints):
        total = total + lax.ppermute(
            density, "kpt", [(i, (i + k) % kpoints) for i in range(kpoints)]
        )
    weight = 1.0 / (kpoints * math.sqrt(count))
    return target[None], total * weight


def solution(mesh):
    in_specs = (P("kpt", "orb", None, None), P())
    out_specs = (P("kpt", "orb", None, None), P("orb", None))
    return jax.shard_map(shards, mesh=mesh, in_specs=in_specs, out_specs=out_specs, check_vma=False)
```

```python
import functools
import math

import jax
import jax.numpy as jnp
import numpy as np
from jax import lax
from jax.experimental import pallas as pl
from jax.experimental.pallas import tpu as pltpu
from jax.sharding import PartitionSpec as P

DEG = 4
ITERS = 8
LANES = 128
COLS = 256
OUT_CHUNKS = 1
BF = jnp.bfloat16
F32 = jnp.float32

filter_centre = 13.0
filter_half = 9.0
margin_eps = 1e-06


def circulant(taps, first, length):
    matrix = np.zeros((length, length))
    for k in range(len(taps)):
        for i in range(length):
            matrix[i, (i + first + k) % length] += taps[k]
    return matrix


def build_tables(size_x, width):
    side = math.isqrt(width)
    kinetic = [math.pi**2 / 6.0 if k == 0 else (-1.0) ** k / (k * k) for k in range(-14, 15)]
    taps = np.array([math.exp(-((k + 0.5) ** 2) / 6.0) for k in range(-8, 8)])
    taps = taps / taps.sum()
    kin_side = circulant(kinetic, -14, side)
    mag_side = circulant(taps, -8, side)
    kin_yz = np.kron(kin_side, np.eye(side)) + np.kron(np.eye(side), kin_side)
    mag_yz = np.kron(mag_side, mag_side)
    return circulant(kinetic, -14, size_x), circulant(taps, -8, size_x), kin_yz, mag_yz


def to_bf16(table):
    return jnp.asarray(np.asarray(table, np.float32)).astype(BF)


def full_spec(array):
    return pl.BlockSpec(array.shape, lambda *_: (0,) * array.ndim)


def filter_kernel(
    in_ref, pot_ref, kx_ref, mx_ref, kyz_ref, myz_ref, myzt_ref, out_ref,
    now, prev, smooth, mixed, back, nxt, fin, mxt_ref, *, first, firstt,
):
    size_x, width = in_ref.shape[1:]
    rows = now.shape[0]
    group = fin.shape[0] // size_x
    step_id = pl.program_id(0)
    blocks = width // COLS
    span = kx_ref.shape[0]
    tiles = [
        (slice(r, r + span), slice(c, c + COLS))
        for c in range(0, width, COLS)
        for r in range(0, rows, span)
    ]
    dot = functools.partial(jnp.dot, preferred_element_type=F32)
    mxt_ref[...] = mx_ref[...].astype(F32).T.astype(BF)
    start = in_ref[...].reshape(rows, width)
    now[:, :width] = start
    now[:, width:] = start
    prev[...] = start

    def window(src, table, n, lead):
        at = (n + lead) % blocks * COLS
        return dot(src[:, at : at + table.shape[0]], table[...])

    def step(j, carry):
        gain = jnp.where(j == 0, 1.0 / filter_half, 2.0 / filter_half).astype(F32)
        keep = jnp.where(j == 0, 0.0, 1.0).astype(F32)
        for n in range(blocks):
            smooth[:, n * COLS : (n + 1) * COLS] = window(now, myz_ref, n, first).astype(BF)
        for rs, cs in tiles:
            value = dot(mx_ref[...], smooth[rs, cs])
            value = value.reshape(span // size_x, size_x, COLS) * pot_ref[:, cs][None]
            mixed[rs, cs] = value.reshape(span, COLS).astype(BF)
        for rs, cs in tiles:
            value = dot(mxt_ref[...], mixed[rs, cs]).astype(BF)
            back[rs, cs] = value
            back[rs, cs.start + width : cs.stop + width] = value
        for n in range(blocks):
            cs = slice(n * COLS, (n + 1) * COLS)
            total = window(now, kyz_ref, n, 0) + window(back, myzt_ref, n, firstt)
            for r in range(0, rows, span):
                rs = slice(r, r + span)
                value = now[rs, cs]
                shifted = total[rs] + dot(kx_ref[...], value) - filter_centre * value.astype(F32)
                nxt[rs, cs] = (gain * shifted - keep * prev[rs, cs].astype(F32)).astype(BF)
        prev[...] = now[:, :width]
        now[:, :width] = nxt[...]
        now[:, width:] = nxt[...]
        return carry

    lax.fori_loop(0, DEG, step, 0)
    fin[pl.ds(pl.multiple_of(step_id * rows, rows), rows), :] = nxt[...]

    @pl.when(step_id == pl.num_programs(0) - 1)
    def _():
        turned = jnp.swapaxes(fin[...].reshape(group, size_x, width), 0, 1)
        out_ref[...] = turned.reshape(out_ref.shape)


def run_filter(orbitals, chunk, chunks, potential, parts, rows):
    size_x, width = orbitals.shape[1:]
    group = orbitals.shape[0] // chunks
    rows = min(rows, group * size_x)
    blocks = width // COLS
    kin_x, mag_x, kin_yz, mag_yz = build_tables(size_x, width)
    span = min(256, rows)
    wide = lambda t: to_bf16(np.kron(np.eye(span // size_x), t))
    piece = lambda t, d: t[:COLS, d % blocks * COLS : (d % blocks + 1) * COLS].T

    def band(t):
        used = [d for d in range(blocks) if np.any(piece(t, d))]
        lead = [d for d in used if (d - 1) % blocks not in used]
        lead = lead[0] if lead else 0
        return lead, to_bf16(np.concatenate([piece(t, lead + i) for i in range(len(used))], 0))

    _, kyz = band(kin_yz)
    first, myz = band(mag_yz)
    firstt, myzt = band(mag_yz.T)
    args = (orbitals, potential, wide(kin_x), wide(mag_x), kyz, myz, myzt)
    per = size_x // parts
    steps = group * size_x // rows
    return pl.pallas_call(
        functools.partial(filter_kernel, first=first, firstt=firstt),
        grid=(steps,),
        in_specs=[
            pl.BlockSpec((rows // size_x, size_x, width), lambda s: (chunk * steps + s, 0, 0))
        ]
        + [full_spec(a) for a in args[1:]],
        out_specs=pl.BlockSpec((parts, per, group, width), lambda s: (0, 0, 0, 0)),
        out_shape=jax.ShapeDtypeStruct((parts, per, group, width), BF),
        scratch_shapes=[
            pltpu.VMEM((rows, 2 * width), BF),
            pltpu.VMEM((rows, width), BF),
            pltpu.VMEM((rows, width), BF),
            pltpu.VMEM((rows, width), BF),
            pltpu.VMEM((rows, 2 * width), BF),
            pltpu.VMEM((rows, width), BF),
            pltpu.VMEM((group * size_x, width), BF),
            pltpu.VMEM((span, span), BF),
        ],
        compiler_params=pltpu.CompilerParams(vmem_limit_bytes=56 << 20),
        cost_estimate=pl.CostEstimate(
            flops=2 * DEG * group * size_x * width
            * (kyz.shape[0] + myz.shape[0] + myzt.shape[0] + 3 * span),
            bytes_accessed=4 * group * size_x * width,
            transcendentals=0,
        ),
        name="chebyshev",
    )(*args)


def triangle(count, side):
    n = count // side
    return [(i, j) for i in range(n) for j in range(i, n)]


def gather_rows(ins, flat):
    start = 0
    for ref in ins:
        size = ref.shape[0] * ref.shape[2]
        flat[start : start + size, :] = (
            ref[:, 0].astype(F32).reshape(size, flat.shape[1]).astype(BF)
        )
        start += size


def margin_kernel(me_ref, *refs, side, gain, order, blocks, sources):
    ins, out_ref, flat, acc = refs[:sources], refs[-3], refs[-2], refs[-1]
    step_id = pl.program_id(0)
    gather_rows(ins, flat)

    @pl.when(step_id == 0)
    def _():
        acc[...] = jnp.zeros_like(acc)

    for i in sorted({i for i, _ in blocks}):
        cols = [j for b, j in blocks if b == i]
        got = lax.dot_general(
            flat[i * side : (i + 1) * side, :],
            flat[cols[0] * side : (cols[-1] + 1) * side, :],
            (((1,), (1,)), ((), ())),
            preferred_element_type=F32,
        )
        for at, j in enumerate(cols):
            row = blocks.index((i, j)) * side
            acc[row : row + side, :] += got[:, at * side : (at + 1) * side]

    @pl.when(step_id == pl.num_programs(0) - 1)
    def _():
        piece = out_ref.shape[1]
        for t, m in enumerate(order):
            rows = pl.multiple_of((me_ref[0] ^ m) * piece, math.gcd(piece, 8))
            out_ref[t] = acc[pl.ds(rows, piece), :] * gain


def run_margin(me, spreads, cells, side, order, blocks, after):
    parts, per, _, width = spreads[0].shape
    count = sum(s.shape[0] * s.shape[2] for s in spreads)
    size = len(blocks) * side
    shape = (parts, size // parts, side)
    return pl.pallas_call(
        functools.partial(
            margin_kernel, side=side, gain=1.0 / cells, order=order, blocks=blocks,
            sources=len(spreads),
        ),
        grid=(per,),
        in_specs=[pl.BlockSpec(memory_space=pltpu.SMEM)]
        + [pl.BlockSpec((parts, 1, s.shape[2], width), lambda x: (0, x, 0, 0)) for s in spreads]
        + [pl.BlockSpec(memory_space=pl.ANY)] * len(after),
        out_specs=pl.BlockSpec(shape, lambda x: (0, 0, 0)),
        out_shape=jax.ShapeDtypeStruct(shape, F32),
        scratch_shapes=[pltpu.VMEM((count, width), BF), pltpu.VMEM((size, side), F32)],
        compiler_params=pltpu.CompilerParams(vmem_limit_bytes=48 << 20),
        cost_estimate=pl.CostEstimate(
            flops=2 * size * side * width * per, bytes_accessed=2 * count * width * per,
            transcendentals=0,
        ),
        name="margin",
    )(me, *spreads, *after)


def stage_masks(parts):
    stages, low = [], 1
    while low < parts:
        bits = [low, 2 * low] if 2 * low < parts else [low]
        masks = [0]
        for b in bits:
            masks += [m ^ b for m in masks]
        stages.append(masks)
        low <<= len(bits)
    return stages


def piece_order(stages):
    order = [0]
    for masks in reversed(stages):
        order = [m ^ o for m in masks for o in order]
    return order


def send(value, mask, parts):
    return lax.ppermute(value, "orb", [(i, i ^ mask) for i in range(parts)])


def scatter_sum(held, stages, parts):
    for masks in stages:
        held = held.reshape((len(masks), -1) + held.shape[1:])
        total = held[0]
        for other in [send(held[i], m, parts) for i, m in enumerate(masks) if i]:
            total = total + other
        held = total
    return held


def gather_pieces(held, stages, parts):
    for masks in reversed(stages):
        got = [send(held, m, parts) for m in masks[1:]]
        held = jnp.concatenate([held] + got, axis=0)
    return held


def split(value):
    high = value.astype(BF)
    return high, (value - high.astype(F32)).astype(BF)


def mul(a, b):
    ah, al = a
    bh, bl = b
    dot = functools.partial(jnp.dot, preferred_element_type=F32)
    return dot(ah, bh) + (dot(ah, bl) + dot(al, bh))


def inverse_root_kernel(
    me_ref, held_ref, out_ref, packed, full, pval, zhi, zlo, *, masks, side, blocks, pieces
):
    me = me_ref[0]
    start = inner = 0
    for piece in pieces:
        for t, m in enumerate(masks):
            rows = pl.multiple_of(start + (me ^ m) * piece, math.gcd(piece, 8))
            packed[pl.ds(rows, piece), :] = held_ref[t, inner : inner + piece]
        start += piece * len(masks)
        inner += piece
    count = full.shape[0]
    for at, (i, j) in enumerate(blocks):
        tile = packed[at * side : (at + 1) * side, :]
        full[i * side : (i + 1) * side, j * side : (j + 1) * side] = tile
        if i != j:
            full[j * side : (j + 1) * side, i * side : (i + 1) * side] = tile.T
    margin = full[...]
    total = jnp.sum(jnp.sum(margin * margin, axis=1, keepdims=True), axis=0, keepdims=True)
    scale = jnp.sqrt(total + margin_eps)
    row = lax.broadcasted_iota(jnp.int32, (count, count), 0)
    col = lax.broadcasted_iota(jnp.int32, (count, count), 1)
    eye = jnp.where(row == col, 1.0, 0.0).astype(F32)

    def factor(ps, p):
        square = mul(ps, ps)
        inner = 6.75 * eye - 2.25 * p + 0.25 * square
        return 0.25 * (9.0 * eye - 9.75 * p + mul(split(square), split(inner)))

    def pair(p, last):
        ps = split(p)
        ws = split(factor(ps, p))
        return ws, None if last else mul(ws, split(mul(ws, ps)))

    ws, pval[...] = pair(margin / scale, False)
    zhi[...], zlo[...] = ws

    def middle(_, carry):
        ws, pval[...] = pair(pval[...], False)
        zhi[...], zlo[...] = split(mul(ws, (zhi[...], zlo[...])))
        return carry

    lax.fori_loop(0, ITERS // 2 - 2, middle, 0)
    ws, _ = pair(pval[...], True)
    z = mul(ws, (zhi[...], zlo[...]))
    out_ref[...] = (z / jnp.sqrt(scale)).astype(BF)


def run_inverse_root(me, held, masks, count, side, blocks, pieces):
    return pl.pallas_call(
        functools.partial(
            inverse_root_kernel, masks=masks, side=side, blocks=blocks, pieces=pieces
        ),
        in_specs=[
            pl.BlockSpec(memory_space=pltpu.SMEM),
            pl.BlockSpec(memory_space=pltpu.VMEM),
        ],
        out_specs=pl.BlockSpec(memory_space=pltpu.VMEM),
        out_shape=jax.ShapeDtypeStruct((count, count), BF),
        scratch_shapes=[
            pltpu.VMEM((len(blocks) * side, side), F32),
            pltpu.VMEM((count, count), F32),
            pltpu.VMEM((count, count), F32),
            pltpu.VMEM((count, count), BF),
            pltpu.VMEM((count, count), BF),
        ],
        compiler_params=pltpu.CompilerParams(vmem_limit_bytes=48 << 20),
        cost_estimate=pl.CostEstimate(
            flops=2 * 51 * count**3, bytes_accessed=4 * count * count, transcendentals=0
        ),
        name="inverse_root",
    )(me, held)


def rotate_kernel(*refs):
    coeff_ref, ins, out_ref, den_ref, flat = refs[0], refs[1:-3], refs[-3], refs[-2], refs[-1]
    parts, _, sets, group, width = out_ref.shape
    gather_rows(ins, flat)
    wide = jnp.dot(coeff_ref[...], flat[...], preferred_element_type=F32)
    wide = wide.astype(BF).astype(F32)
    for c in range(sets):
        own = wide[c * parts * group : (c + 1) * parts * group].reshape(parts, group, width)
        out_ref[:, 0, c] = own.astype(BF)
    den_ref[...] = jnp.sum(wide * wide, axis=0)[None, None]


def run_rotate(coeff, spreads):
    parts, per, group, width = spreads[0].shape
    own, count = coeff.shape
    sets = own // (parts * group)
    return pl.pallas_call(
        rotate_kernel,
        grid=(per,),
        in_specs=[full_spec(coeff)]
        + [pl.BlockSpec((parts, 1, s.shape[2], width), lambda x: (0, x, 0, 0)) for s in spreads],
        out_specs=[
            pl.BlockSpec((parts, 1, sets, group, width), lambda x: (0, x, 0, 0, 0)),
            pl.BlockSpec((1, 1, width), lambda x: (x, 0, 0)),
        ],
        out_shape=[
            jax.ShapeDtypeStruct((parts, per, sets, group, width), BF),
            jax.ShapeDtypeStruct((per, 1, width), F32),
        ],
        scratch_shapes=[pltpu.VMEM((count, width), BF)],
        compiler_params=pltpu.CompilerParams(vmem_limit_bytes=48 << 20),
        cost_estimate=pl.CostEstimate(
            flops=2 * count * own * width * per,
            bytes_accessed=2 * (count + own) * width * per,
            transcendentals=0,
        ),
        name="rotate",
    )(coeff, *spreads)


def restore_kernel(*refs):
    in_ref, out_ref = refs[0], refs[-1]
    _, _, sets, group, width = in_ref.shape
    rows = out_ref.shape[1]
    wide = in_ref[...].astype(F32).reshape(rows, sets * group, width)
    out_ref[...] = jnp.swapaxes(wide, 0, 1).astype(BF)


def run_restore(spread, target, chunk, chunks):
    parts, per, sets, group, width = spread.shape
    own, size_x = sets * group, parts * per
    rows = max(16, per)
    args = (spread,) if target is None else (spread, target)
    return pl.pallas_call(
        restore_kernel,
        grid=(size_x // rows,),
        in_specs=[
            pl.BlockSpec((rows // per, per, sets, group, width), lambda x: (x, 0, 0, 0, 0))
        ]
        + [pl.BlockSpec(memory_space=pl.ANY)] * (len(args) - 1),
        out_specs=pl.BlockSpec((own, rows, width), lambda x: (chunk, x, 0)),
        out_shape=jax.ShapeDtypeStruct((own * chunks, size_x, width), BF),
        input_output_aliases={} if target is None else {1: 0},
        compiler_params=pltpu.CompilerParams(vmem_limit_bytes=48 << 20),
        cost_estimate=pl.CostEstimate(
            flops=0, bytes_accessed=4 * own * size_x * width, transcendentals=0
        ),
        name="restore",
    )(*args)


def shards(orbitals, potential):
    parts = lax.axis_size("orb")
    mine, size_x, width = orbitals.shape[1:]
    chunks = max(1, mine // 8)
    outs = min(chunks, OUT_CHUNKS)
    count = mine * parts
    exchange = lambda v: lax.all_to_all(v, "orb", split_axis=0, concat_axis=0, tiled=True)
    me = lax.axis_index("orb").astype(jnp.int32).reshape(1)
    stages = stage_masks(parts)
    order = piece_order(stages)
    spreads = [
        exchange(run_filter(orbitals[0], c, chunks, potential, parts, 512))
        for c in range(chunks)
    ]
    early = (chunks - 1) * (count // chunks)
    blocks = triangle(early, LANES)
    last = [pair for pair in triangle(count, LANES) if pair not in blocks]
    helds = []
    for some, ready in ((blocks, spreads[:-1]), (last, spreads)):
        if some:
            partial = run_margin(me, ready, size_x * width, LANES, order, some, helds)
            helds.append(scatter_sum(partial, stages[:1], parts))
    held = scatter_sum(jnp.concatenate(helds, axis=1), stages[1:], parts)
    held = gather_pieces(held, stages, parts)
    pieces = [h.shape[1] for h in helds]
    coeff = run_inverse_root(me, held, order, count, LANES, blocks + last, pieces)
    own = count // outs
    target = None
    density = 0.0
    returned = []
    for c in range(outs):
        rotated, part = run_rotate(coeff[c * own : (c + 1) * own], spreads)
        returned.append(exchange(rotated))
        density = density + part[:, 0]
    for c in range(outs):
        target = run_restore(returned[c], target, c, outs)
    kpoints = lax.axis_size("kpt")
    total = density
    for k in range(1, kpoints):
        total = total + lax.ppermute(
            density, "kpt", [(i, (i + k) % kpoints) for i in range(kpoints)]
        )
    weight = 1.0 / (kpoints * math.sqrt(count))
    return target[None], total * weight


def solution(mesh):
    in_specs = (P("kpt", "orb", None, None), P())
    out_specs = (P("kpt", "orb", None, None), P("orb", None))
    return jax.shard_map(shards, mesh=mesh, in_specs=in_specs, out_specs=out_specs, check_vma=False)
```
